128 devices in a mesh: wrap: 16 (over y_lo, z, core), span: 8 (over x, y_hi).
Axes of the slice: x: 4, y: 4 (y_hi: 2, y_lo: 2; y = y_hi * 2 + y_lo), z: 4, core: 2. Of those that a mesh axis runs over, the one named last changes fastest.
Arguments:
- adjoint_start: float32 [5, 32, 256, 1024], P(None, None, 'wrap', 'span'), may hold values from -6 to 6
- adjoint_source: float32 [5, 32, 256, 1024], P(None, None, 'wrap', 'span'), may hold values from -6 to 6
- jacobians: bfloat16 [3, 5, 5, 32, 256, 1024], P(None, None, None, None, 'wrap', 'span'), may hold values from -1.1953125 to 1.1953125
- dissipation: float32 [32, 256, 1024], P(None, 'wrap', 'span'), may hold values from 0.5 to 2
- wall_mask: int32 [256, 1024], P('wrap', 'span'), may hold values from 0 to 1, as said below
- wake_partner: int32 [256, 1024], P('wrap', 'span'), may hold values from 0 to 255, as said below
- surface_slopes: float32 [3, 5, 256, 1024], P(None, None, 'wrap', 'span'), may hold values from -2.5 to 2.5
- control_points: int32 [4, 256, 1024], P(None, 'wrap', 'span'), may hold values from 0 to 1023
- control_weights: float32 [4, 256, 1024], P(None, 'wrap', 'span'), may hold values from 0.02 to 0.1
Outputs:
- adjoint_final: float32 [5, 32, 256, 1024], P(None, None, 'wrap', 'span')
- residual: float32 [5, 32, 256, 1024], P(None, None, 'wrap', 'span')
- shape_gradient: float32 [3, 1024], P(None, ('wrap', 'span'))
The draws below stay inside these ranges and needn't reach their ends.
Inputs may be any that keep to these rules, and one draw needn't show every extreme that they name: `wall_mask`: 1 marks wall, 0 the wake cut; the wall covers one middle range of the wrap index and the span indices below a tip index; both kinds occur. wake_partner[i, k] lies within 1 of 255 - i, and equals it at i = 0 and i = 255.
All inputs are finite; a program needn't handle non-finite values.
Results may differ from the reference program's by a relative error of at most 0.0003.
Values sent between devices are 32-bit elements; how exact they have to be, the bound alone decides.
No kernel may reach another device: no remote copies, remote signals or barrier semaphores. Data moves between devices by JAX's collectives and lax.ppermute only.
A program may use at most 128 MiB of HBM per device.

```python
import math
import jax
import jax.numpy as jnp

NJ = 32
LISTS = 4
SWEEPS = 2
NI = 256
NK = 1024
NCP = 1024


def draw_wall_mask(key, part):
    first_key, second_key = jax.random.split(key)
    start = jax.random.randint(first_key, (), NI // 8, NI // 4 + 1)
    tip = jax.random.randint(second_key, (), NK // 2, 3 * NK // 4 + 1)
    wrap_index = jnp.arange(NI)[:, None]
    span_index = jnp.arange(NK)[None, :]
    inside = (wrap_index >= start) & (wrap_index < NI - start) & (span_index < tip)
    return inside.astype(jnp.int32)


def draw_wake_partner(key, part):
    offsets = jax.random.randint(key, (NI, NK), -1, 2)
    wrap_index = jnp.arange(NI)[:, None]
    offsets = jnp.where((wrap_index == 0) | (wrap_index == NI - 1), 0, offsets)
    return (NI - 1 - wrap_index + offsets).astype(jnp.int32)


def set_ends(values, key, low, top_value):
    longest = values.shape.index(max(values.shape))
    spots = []
    for shift in (0, 1):
        where = [jax.random.randint(jax.random.fold_in(key, axis), (), 0, length) for axis, length in enumerate(values.shape)]
        where[longest] = (where[longest] + shift) % values.shape[longest]
        spots.append(tuple(where))
    return values.at[spots[0]].set(low).at[spots[1]].set(top_value)


def level_of(own_key, dims, pieces, low, largest):
    factor_of = 1.0
    for axis_at, parts in pieces:
        draws = jax.random.uniform(jax.random.fold_in(jax.random.fold_in(own_key, 6), axis_at), (parts,), jnp.float32, low / len(pieces), largest / len(pieces))
        factor_of = factor_of * jnp.repeat(jnp.exp(draws), dims[axis_at] // parts).reshape((-1,) + (1,) * (len(dims) - 1 - axis_at))
    return factor_of


def normal_values(rng, dims, width, limit, pieces=(), dtype=jnp.bfloat16):
    level = level_of(rng, dims, pieces, -0.22, 0.18) if pieces else 1.0
    values = jax.random.normal(rng, dims, jnp.float32) * width * level
    return jnp.minimum(jnp.maximum(values, -limit), limit).astype(dtype)


def setup_inputs(seed: int = 0) -> dict:
    streams_of = jax.random.split(jax.random.key(seed), 10)
    return {
        "adjoint_start": normal_values(streams_of[0], (5, NJ, NI, NK), 1.0, 6.0, ((2, 16), (3, 8)), jnp.float32),
        "adjoint_source": normal_values(streams_of[1], (5, NJ, NI, NK), 1.0, 6.0, ((2, 16), (3, 8)), jnp.float32),
        "jacobians": normal_values(streams_of[2], (3, 5, 5, NJ, NI, NK), 0.2, 1.1953125, ((4, 16), (5, 8))),
        "dissipation": jnp.clip(jnp.exp(math.log(2.0) - 1.3862944 * jax.random.uniform(streams_of[3], (NJ, NI, NK), jnp.float32) ** level_of(streams_of[3], (NJ, NI, NK), ((1, 16), (2, 8)), -0.2, 0.2)), 0.5, 2.0),
        "wall_mask": draw_wall_mask(jax.random.fold_in(streams_of[9], 71), 0),
        "wake_partner": draw_wake_partner(jax.random.fold_in(streams_of[9], 71), 0),
        "surface_slopes": normal_values(streams_of[6], (3, 5, NI, NK), 5 ** -0.5, 2.5, ((2, 16), (3, 8)), jnp.float32),
        "control_points": set_ends(jax.random.randint(streams_of[7], (LISTS, NI, NK), 0, NCP), jax.random.fold_in(streams_of[7], 1), 0, NCP - 1).astype(jnp.int32),
        "control_weights": jnp.clip(0.02 + 0.08 * jax.random.uniform(streams_of[8], (LISTS, NI, NK), jnp.float32) ** level_of(streams_of[8], (LISTS, NI, NK), ((1, 16), (2, 8)), -0.2, 0.2), 0.02, 0.1),
    }


OMEGA = 0.8


def neighbours(adjoint, wall_mask, wake_partner):
    next_wrap = jnp.roll(adjoint, -1, axis=2)
    prev_wrap = jnp.roll(adjoint, 1, axis=2)
    zeros_span = jnp.zeros_like(adjoint[..., :1])
    next_span = jnp.concatenate([adjoint[..., 1:], zeros_span], axis=3)
    prev_span = jnp.concatenate([zeros_span, adjoint[..., :-1]], axis=3)
    bottom = adjoint[:, 0]
    index_table = jnp.broadcast_to(wake_partner[None], bottom.shape)
    across = jnp.take_along_axis(bottom, index_table, axis=1)
    ghost_cells = jnp.where(wall_mask[None] == 1, bottom, across)
    zero_normal = jnp.zeros_like(adjoint[:, :1])
    next_normal = jnp.concatenate([adjoint[:, 1:], zero_normal], axis=1)
    prev_normal = jnp.concatenate([ghost_cells[:, None], adjoint[:, :-1]], axis=1)
    return ((next_wrap, prev_wrap), (next_normal, prev_normal), (next_span, prev_span))


def apply_operator(adjoint, jacobians, dissipation, wall_mask, wake_partner):
    pairs = neighbours(adjoint, wall_mask, wake_partner)
    damping = (2.0 * adjoint - pairs[0][0] - pairs[0][1]) + (2.0 * adjoint - pairs[1][0] - pairs[1][1]) + (2.0 * adjoint - pairs[2][0] - pairs[2][1])
    result = dissipation[None] * damping
    for direction in range(3):
        difference = pairs[direction][0] - pairs[direction][1]
        blocks = [jnp.sum(jacobians[direction, component].astype(jnp.float32) * difference, axis=0) for component in range(5)]
        result = result + jnp.stack(blocks)
    return result


def reference(adjoint_start, adjoint_source, jacobians, dissipation, wall_mask, wake_partner, surface_slopes, control_points, control_weights):
    adjoint = adjoint_start
    for sweep in range(SWEEPS):
        update = adjoint_source - apply_operator(adjoint, jacobians, dissipation, wall_mask, wake_partner)
        adjoint = adjoint + OMEGA * update / (6.0 * dissipation[None])
    residual = adjoint_source - apply_operator(adjoint, jacobians, dissipation, wall_mask, wake_partner)
    wall_row = adjoint[:, 0]
    surface_grad = jnp.sum(surface_slopes * wall_row[None], axis=1) * wall_mask[None].astype(jnp.float32)
    values = surface_grad[None] * control_weights[:, None]
    values = jnp.moveaxis(values, 1, -1).reshape(-1, 3)
    summed = jax.ops.segment_sum(values, control_points.reshape(-1), num_segments=NCP)
    return adjoint, residual, summed.T
```

```python
import functools

import jax
import jax.numpy as jnp
from jax import lax
from jax.experimental import pallas as pl
from jax.experimental.pallas import tpu as pltpu
from jax.sharding import PartitionSpec as P

COMPS = 5
NJ = 32
ROWS = 16
LANES = 128
HALF = 8
WRAP = 16
SPAN = 8
LISTS = 4
OMEGA = 0.8
F32 = jnp.float32
BF16 = jnp.bfloat16
VSPEC = pl.BlockSpec(memory_space=pltpu.VMEM)


def shape_of(*dims, dtype=F32):
    return jax.ShapeDtypeStruct(dims, dtype)


FARSPEC = pl.BlockSpec(memory_space=pltpu.HBM)


def run_kernel(
    kernel,
    outs,
    args,
    scratch=(),
    aliases=None,
    flops=0,
    name=None,
    far=(),
    far_out=(),
    vmem=4,
):
    moved = sum(a.size * a.dtype.itemsize for a in args)
    return pl.pallas_call(
        kernel,
        out_shape=outs,
        in_specs=[FARSPEC if n in far else VSPEC for n in range(len(args))],
        out_specs=[FARSPEC if n in far_out else VSPEC for n in range(len(outs))],
        scratch_shapes=list(scratch),
        input_output_aliases=aliases or {},
        compiler_params=pltpu.CompilerParams(vmem_limit_bytes=int(vmem * 2**20)),
        cost_estimate=pl.CostEstimate(flops=flops, transcendentals=0, bytes_accessed=moved),
        name=name,
    )(*args)


def lane_index():
    return lax.broadcasted_iota(jnp.int32, (HALF, LANES), 1)


def row_index():
    return lax.broadcasted_iota(jnp.int32, (HALF, LANES), 0)


def spread(row):
    return jnp.broadcast_to(row, (HALF, LANES))


def pack_edges(packed, halves, j, lane):
    for half in range(2):
        m = 2 * j + half
        here = (lane >> 1) == m
        for c in range(COMPS):
            packed[c] = jnp.where(here, pltpu.roll(halves[c][half], 2 * m + 1, 1), packed[c])
    return packed


def first_faces(start_ref, v_ref, slab_ref, low_ref, high_ref, edge_ref, sem):
    lane = lane_index()
    copy = pltpu.make_async_copy(start_ref, v_ref.at[:, :NJ], sem)
    copy.start()
    for c in range(COMPS):
        v_ref[c, NJ] = jnp.zeros((ROWS, LANES), F32)
    copy.wait()

    def step(j, packed):
        halves = [(v_ref[c, j, :HALF], v_ref[c, j, HALF:]) for c in range(COMPS)]
        for c in range(COMPS):
            low_ref[c, pl.ds(j, 1)] = halves[c][0][:1]
            high_ref[c, pl.ds(j, 1)] = halves[c][1][HALF - 1 :]
        return tuple(pack_edges(list(packed), halves, j, lane))

    packed = lax.fori_loop(
        0, NJ, step, tuple(jnp.zeros((HALF, LANES), F32) for _ in range(COMPS)), unroll=4
    )
    for c in range(COMPS):
        edge_ref[c] = packed[c]
        slab_ref[c] = v_ref[c, 0]


def mirror_rows(slab_ref, before_ref, after_ref, out_ref):
    for c in range(COMPS):
        out_ref[c, 0:1] = after_ref[c, 0:1]
        for i in range(ROWS):
            out_ref[c, i + 1 : i + 2] = slab_ref[c, ROWS - 1 - i : ROWS - i]
        out_ref[c, ROWS + 1 : ROWS + 2] = before_ref[c, 0:1]
        out_ref[c, ROWS + 2 :] = jnp.zeros((24 - ROWS - 2, LANES), F32)


CHUNK = 4
CHUNKS = NJ // CHUNK
AHEAD = 3


def apply_blocks(stage, *refs):
    last = stage == 2
    (v_ref, slab_ref, jac_ref, src_ref, dis_ref, before_ref, after_ref, down_ref, up_ref) = refs[:9]
    if stage == 0:
        out_ref, part_ref, low_ref, high_ref, edge_ref, wide_ref, base_ref = refs[9:16]
        q_ref, narrow_ref, sems = refs[16:]
    elif stage == 1:
        out_ref, part_ref, low_ref, high_ref, edge_ref, q_ref = refs[9:]
    else:
        far_ref, part_ref, final_ref, q_ref, out_ref, sems = refs[9:]

    def block_copy(n):
        at = pl.ds(n * CHUNK, CHUNK)
        return pltpu.make_async_copy(
            jac_ref.at[:, :, :, at], narrow_ref.at[:, :, :, at], sems.at[n]
        )

    def result_copy(n):
        at = pl.ds(n * CHUNK, CHUNK)
        return pltpu.make_async_copy(out_ref.at[:, at], far_ref.at[:, at], sems.at[n])

    if stage == 0:
        for n in range(AHEAD):
            block_copy(n).start()
    if last:
        final_copies = (
            pltpu.make_async_copy(v_ref.at[:, 1:NJ], final_ref.at[:, 1:], sems.at[CHUNKS]),
            pltpu.make_async_copy(slab_ref, final_ref.at[:, 0], sems.at[CHUNKS + 1]),
        )
        for copy in final_copies:
            copy.start()
    lane, row = lane_index(), row_index()
    place = lax.axis_index("span")
    has_down, has_up = place > 0, place < SPAN - 1
    even = (lane & 1) == 0
    for c in range(COMPS):
        from_up = jnp.where(has_up, pltpu.roll(up_ref[c], LANES - 1, 1), 0.0)
        from_down = jnp.where(has_down, pltpu.roll(down_ref[c], 1, 1), 0.0)
        q_ref[c] = jnp.where(even, from_up, from_down)
        if not last:
            out_ref[c, NJ] = jnp.zeros((ROWS, LANES), F32)
    first_lane, last_lane = lane == 0, lane == LANES - 1
    first_row, last_row = row == 0, row == HALF - 1

    def cells(c, j, half):
        at = slice(half * HALF, (half + 1) * HALF)
        if isinstance(j, int) and j < 0:
            return jnp.zeros((HALF, LANES), F32)
        if isinstance(j, int) and j == 0:
            return slab_ref[c, at]
        return v_ref[c, j, at]

    def step(j, packed):
        at_row = pl.ds(j, 1)
        dis = (dis_ref[j, :HALF], dis_ref[j, HALF:])
        diffs = [[None] * COMPS for _ in range(3)]
        sums, here = [], []
        for c in range(COMPS):
            a, b = cells(c, j, 0), cells(c, j, 1)
            here.append((a, b))
            before = spread(before_ref[c, at_row])
            after = spread(after_ref[c, at_row])
            a_up, b_up = pltpu.roll(a, HALF - 1, 0), pltpu.roll(b, HALF - 1, 0)
            a_dn, b_dn = pltpu.roll(a, 1, 0), pltpu.roll(b, 1, 0)
            next_i = (jnp.where(last_row, b_up, a_up), jnp.where(last_row, after, b_up))
            prev_i = (jnp.where(first_row, before, a_dn), jnp.where(first_row, a_dn, b_dn))
            if last and isinstance(j, int) and j == NJ - 1:
                next_j = tuple(jnp.zeros((HALF, LANES), F32) for _ in range(2))
            else:
                next_j = tuple(cells(c, j + 1, half) for half in range(2))
            prev_j = tuple(cells(c, j - 1, half) for half in range(2))
            next_k, prev_k = [], []
            for half, x in enumerate((a, b)):
                edge = pltpu.roll(q_ref[c], LANES - 1 - 4 * j - 2 * half, 1)
                next_k.append(jnp.where(last_lane, edge, pltpu.roll(x, LANES - 1, 1)))
                prev_k.append(jnp.where(first_lane, edge, pltpu.roll(x, 1, 1)))
            for d, (nxt, prv) in enumerate(((next_i, prev_i), (next_j, prev_j), (next_k, prev_k))):
                diffs[d][c] = tuple(n - p for n, p in zip(nxt, prv))
            sums.append(
                tuple(
                    (next_i[half] + prev_i[half])
                    + (next_j[half] + prev_j[half])
                    + (next_k[half] + prev_k[half])
                    for half in range(2)
                )
            )
        halves = []
        weight = None if last else tuple((OMEGA / 6.0) / d for d in dis)
        for c in range(COMPS):
            acc = [jnp.zeros((HALF, LANES), F32), jnp.zeros((HALF, LANES), F32)]
            for d in range(3):
                for b in range(COMPS):
                    if stage == 0:
                        block = narrow_ref[d, c, b, j].astype(F32)
                        wide_ref[d, c, b, j] = block
                        if d == 1 and isinstance(j, int) and j == 0:
                            base_ref[c, b] = block
                    else:
                        block = jac_ref[d, c, b, j]
                    acc[0] = acc[0] + block[:HALF] * diffs[d][b][0]
                    acc[1] = acc[1] + block[HALF:] * diffs[d][b][1]
            rest = []
            for half in range(2):
                x, total = here[c][half], sums[c][half]
                rhs = src_ref[c, j, half * HALF : (half + 1) * HALF] - acc[half]
                if last:
                    rest.append(rhs - dis[half] * (6.0 * x - total))
                else:
                    rest.append(
                        ((1.0 - OMEGA) * x + (OMEGA / 6.0) * total) + weight[half] * rhs
                    )
            if isinstance(j, int) and j == 0:
                part_ref[c, :HALF] = rest[0]
                part_ref[c, HALF:] = rest[1]
            out_ref[c, j, :HALF] = rest[0]
            out_ref[c, j, HALF:] = rest[1]
            if not last:
                low_ref[c, at_row] = rest[0][:1]
                high_ref[c, at_row] = rest[1][HALF - 1 :]
            halves.append(rest)
        if last:
            return packed
        return tuple(pack_edges(list(packed), halves, j, lane))

    def loop_step(j, packed):
        if stage == 0:

            @pl.when(j % CHUNK == 0)
            def _():
                n = j // CHUNK
                block_copy(n).wait()

                @pl.when(n + AHEAD < CHUNKS)
                def _():
                    block_copy(n + AHEAD).start()

        packed = step(j, packed)
        if last:

            @pl.when(j % CHUNK == CHUNK - 1)
            def _():
                result_copy(j // CHUNK).start()

        return packed

    packed = () if last else tuple(jnp.zeros((HALF, LANES), F32) for _ in range(COMPS))
    if stage == 0:
        block_copy(0).wait()
        block_copy(AHEAD).start()
    packed = step(0, packed)
    packed = step(1, packed)
    packed = lax.fori_loop(2, NJ, loop_step, packed)
    if last:
        for n in range(CHUNKS):
            result_copy(n).wait()
        for copy in final_copies:
            copy.wait()
    else:
        for c in range(COMPS):
            edge_ref[c] = packed[c]


def add_ghosts(last, *refs):
    (slab_ref, base_ref, dis_ref, wall_ref, partner_ref, window_ref, part_ref) = refs[:7]
    if last:
        _, far_ref, out_ref, sem = refs[7:]
    else:
        low_in, high_in, edge_in, out_ref, low_ref, high_ref, edge_ref = refs[7:]
        low_ref[...] = low_in[...]
        high_ref[...] = high_in[...]
    lane = lane_index()
    base = lax.axis_index("wrap") * ROWS
    row = lax.broadcasted_iota(jnp.int32, (ROWS, LANES), 0)
    shift = partner_ref[...] - (WRAP * ROWS - 1 - base - row)
    wall = wall_ref[...] == 1
    dis = dis_ref[0]
    ghosts = []
    for c in range(COMPS):
        rows = window_ref[c]
        lower, middle, upper = rows[:ROWS], rows[1 : ROWS + 1], rows[2 : ROWS + 2]
        chosen = jnp.where(shift == -1, upper, jnp.where(shift == 1, lower, middle))
        ghosts.append(jnp.where(wall, slab_ref[c], chosen))
    if not last:
        weight = (OMEGA / 6.0) / dis
    for c in range(COMPS):
        total = base_ref[c, 0] * ghosts[0]
        for b in range(1, COMPS):
            total = total + base_ref[c, b] * ghosts[b]
        if last:
            fresh = part_ref[c] + (dis * ghosts[c] + total)
        else:
            fresh = part_ref[c] + ((OMEGA / 6.0) * ghosts[c] + weight * total)
        out_ref[c] = fresh
        if not last:
            low_ref[c, 0:1] = fresh[:1]
            high_ref[c, 0:1] = fresh[ROWS - 1 :]
            edge = jnp.where(lane < 2, pltpu.roll(fresh[:HALF], 1, 1), edge_in[c])
            here = (lane == 2) | (lane == 3)
            edge_ref[c] = jnp.where(here, pltpu.roll(fresh[HALF:], 3, 1), edge)
    if last:
        copy = pltpu.make_async_copy(out_ref, far_ref.at[:, 0], sem)
        copy.start()
        copy.wait()


POINT_LANES = 64


def surface_sums(*refs):
    slab_ref, slope_ref, wall_ref, points_ref, weights_ref = refs[:5]
    kept_ref, sent_ref, left_ref, right_ref, sum_ref = refs[5:]
    wall = wall_ref[...].astype(F32)
    grads = []
    for x in range(3):
        total = slope_ref[x, 0] * slab_ref[0]
        for a in range(1, COMPS):
            total = total + slope_ref[x, a] * slab_ref[a]
        grads.append(total * wall)
    owner = lax.broadcasted_iota(jnp.int32, (WRAP, LANES), 0)
    inner = lax.broadcasted_iota(jnp.int32, (POINT_LANES, LANES), 0)
    for slot in range(LISTS):
        points = points_ref[slot]
        scale = weights_ref[slot]
        major, minor = points >> 6, points & (POINT_LANES - 1)
        parts = []
        for x in range(3):
            value = grads[x] * scale
            high = value.astype(BF16).astype(F32)
            parts.append((high, value - high))
        for i in range(ROWS):
            at = pl.ds((slot * ROWS + i) * LANES, LANES)
            mine = owner == jnp.broadcast_to(major[i : i + 1], (WRAP, LANES))
            for x in range(3):
                for part in range(2):
                    value = jnp.broadcast_to(parts[x][part][i : i + 1], (WRAP, LANES))
                    left_ref[x * 2 + part, :, at] = jnp.where(mine, value, 0.0).astype(BF16)
            same = inner == jnp.broadcast_to(minor[i : i + 1], (POINT_LANES, LANES))
            right_ref[:, at] = jnp.where(same, 1.0, 0.0).astype(BF16)
    left = left_ref[...].reshape(6 * WRAP, LISTS * ROWS * LANES)
    product = lax.dot_general(
        left, right_ref[...], (((1,), (1,)), ((), ())), preferred_element_type=F32
    )
    sum_ref[...] = jnp.zeros_like(sum_ref)
    for x in range(3):
        first = product[2 * x * WRAP : (2 * x + 1) * WRAP]
        second = product[(2 * x + 1) * WRAP : (2 * x + 2) * WRAP]
        both = first + second
        for w in range(WRAP):
            sum_ref[w, x : x + 1, :POINT_LANES] = both[w : w + 1]
    mine = lax.axis_index("wrap") & 1
    for n in range(WRAP // 2):
        kept_ref[n] = sum_ref[2 * n + mine]
        sent_ref[n] = sum_ref[2 * n + 1 - mine]


def halve(bit, kept_in, got_ref, kept_ref, sent_ref, sum_ref):
    sum_ref[...] = kept_in[...] + got_ref[...]
    mine = (lax.axis_index("wrap") >> bit) & 1
    for n in range(kept_ref.shape[0]):
        kept_ref[n] = sum_ref[2 * n + mine]
        sent_ref[n] = sum_ref[2 * n + 1 - mine]


def add_tiles(a_ref, b_ref, out_ref):
    out_ref[...] = a_ref[...] + b_ref[...]


def finish_points(a_ref, b_ref, out_ref):
    total = a_ref[0] + b_ref[0]
    out_ref[...] = pltpu.roll(total, LANES - 8 * lax.axis_index("span"), 1)[:3, :8]


def reduce_points(kept, sent):
    for bit in range(4):
        got = lax.ppermute(sent, "wrap", [(i, i ^ (1 << bit)) for i in range(WRAP)])
        count = kept.shape[0]
        if bit < 3:
            kept, sent = run_kernel(
                functools.partial(halve, bit + 1),
                [shape_of(count // 2, HALF, LANES)] * 2,
                (kept, got),
                scratch=(pltpu.VMEM((count, HALF, LANES), F32),),
                name="halve",
            )
        else:
            (kept,) = run_kernel(add_tiles, [shape_of(1, HALF, LANES)], (kept, got), name="add")
    for bit in range(3):
        got = lax.ppermute(kept, "span", [(i, i ^ (1 << bit)) for i in range(SPAN)])
        if bit < 2:
            (kept,) = run_kernel(add_tiles, [shape_of(1, HALF, LANES)], (kept, got), name="add")
    (out,) = run_kernel(finish_points, [shape_of(3, 8)], (kept, got), name="points")
    return out


WRAP_UP = [(i, (i + 1) % WRAP) for i in range(WRAP)]
WRAP_DOWN = [(b, a) for a, b in WRAP_UP]
SPAN_UP = [(i, (i + 1) % SPAN) for i in range(SPAN)]
SPAN_DOWN = [(b, a) for a, b in SPAN_UP]
MIRROR = [(i, WRAP - 1 - i) for i in range(WRAP)]

FIELD = (COMPS, NJ, ROWS, LANES)
TALL = (COMPS, NJ + 1, ROWS, LANES)
SLAB = (COMPS, ROWS, LANES)
FACE = (COMPS, NJ, LANES)
EDGE = (COMPS, HALF, LANES)
BLOCKS = (3, COMPS, COMPS, NJ, ROWS, LANES)
SWEEP_FLOPS = 160 * COMPS * NJ * ROWS * LANES
DMA = pltpu.SemaphoreType.DMA


def exchange(slab, low, high, edge):
    before = lax.ppermute(high, "wrap", WRAP_UP)
    after = lax.ppermute(low, "wrap", WRAP_DOWN)
    down = lax.ppermute(edge, "span", SPAN_UP)
    up = lax.ppermute(edge, "span", SPAN_DOWN)
    (rows,) = run_kernel(
        mirror_rows, [shape_of(COMPS, 24, LANES)], (slab, before, after), name="mirror"
    )
    window = lax.ppermute(rows, "wrap", MIRROR)
    return (before, after, down, up), window


def operator_step(stage, v, slab, faces, blocks, base, fixed):
    source, dissipation, wall, partner = fixed
    halos, window = exchange(slab, *faces)
    args = (v, slab, blocks, source, dissipation, *halos)
    kernel = functools.partial(apply_blocks, stage)
    if stage < 2:
        outs = [shape_of(*d) for d in (TALL, SLAB, FACE, FACE, EDGE)]
        scratch = [pltpu.VMEM(EDGE, F32)]
        if stage == 0:
            outs += [shape_of(*BLOCKS), shape_of(*BLOCKS[1:3], ROWS, LANES)]
            scratch += [pltpu.VMEM(BLOCKS, BF16), DMA((CHUNKS,))]
        v, part, *rest = run_kernel(
            kernel,
            outs,
            args,
            scratch=scratch,
            flops=SWEEP_FLOPS,
            name="blocks",
            far=(2,) if stage == 0 else (),
            vmem=12 if stage == 0 else 4,
        )
        if stage == 0:
            *rest, blocks, base = rest
        slab, *faces = run_kernel(
            functools.partial(add_ghosts, False),
            [shape_of(*d) for d in (SLAB, FACE, FACE, EDGE)],
            (slab, base, dissipation, wall, partner, window, part, *rest),
            flops=1000000,
            name="ghosts",
        )
        return v, slab, faces, blocks, base
    residual, part, final = run_kernel(
        kernel,
        [shape_of(*FIELD), shape_of(*SLAB), shape_of(*FIELD)],
        args,
        scratch=(pltpu.VMEM(EDGE, F32), pltpu.VMEM(FIELD, F32), DMA((CHUNKS + 2,))),
        flops=SWEEP_FLOPS,
        name="blocks",
        far_out=(0, 2),
    )
    (residual,) = run_kernel(
        functools.partial(add_ghosts, True),
        [shape_of(*FIELD)],
        (slab, base, dissipation, wall, partner, window, part, residual),
        scratch=(pltpu.VMEM(SLAB, F32), DMA),
        aliases={7: 0},
        flops=1000000,
        name="ghosts",
        far=(7,),
        far_out=(0,),
    )
    return final, residual


def shards(
    adjoint_start,
    adjoint_source,
    jacobians,
    dissipation,
    wall_mask,
    wake_partner,
    surface_slopes,
    control_points,
    control_weights,
):
    fixed = (adjoint_source, dissipation, wall_mask, wake_partner)
    v, slab, *faces = run_kernel(
        first_faces,
        [shape_of(*d) for d in (TALL, SLAB, FACE, FACE, EDGE)],
        (pltpu.with_memory_space_constraint(adjoint_start, pltpu.HBM),),
        scratch=(DMA,),
        flops=1000000,
        name="faces",
        far=(0,),
    )
    blocks, base = pltpu.with_memory_space_constraint(jacobians, pltpu.HBM), None
    for stage in range(2):
        v, slab, faces, blocks, base = operator_step(stage, v, slab, faces, blocks, base, fixed)
    kept, sent = run_kernel(
        surface_sums,
        [shape_of(WRAP // 2, HALF, LANES)] * 2,
        (slab, surface_slopes, wall_mask, control_points, control_weights),
        scratch=(
            pltpu.VMEM((6, WRAP, LISTS * ROWS * LANES), BF16),
            pltpu.VMEM((POINT_LANES, LISTS * ROWS * LANES), BF16),
            pltpu.VMEM((WRAP, HALF, LANES), F32),
        ),
        flops=10000000,
        name="surface",
        vmem=8,
    )
    shape_gradient = reduce_points(kept, sent)
    final, residual = operator_step(2, v, slab, faces, blocks, base, fixed)
    return final, residual, shape_gradient


def solution(mesh):
    in_specs = (
        P(None, None, "wrap", "span"),
        P(None, None, "wrap", "span"),
        P(None, None, None, None, "wrap", "span"),
        P(None, "wrap", "span"),
        P("wrap", "span"),
        P("wrap", "span"),
        P(None, None, "wrap", "span"),
        P(None, "wrap", "span"),
        P(None, "wrap", "span"),
    )
    out_specs = (
        P(None, None, "wrap", "span"),
        P(None, None, "wrap", "span"),
        P(None, ("wrap", "span")),
    )
    return jax.shard_map(shards, mesh=mesh, in_specs=in_specs, out_specs=out_specs, check_vma=False)
```

```python
import functools

import jax
import jax.numpy as jnp
from jax import lax
from jax.experimental import pallas as pl
from jax.experimental.pallas import tpu as pltpu
from jax.sharding import PartitionSpec as P

COMPS = 5
NJ = 32
ROWS = 16
LANES = 128
HALF = 8
WRAP = 16
SPAN = 8
LISTS = 4
OMEGA = 0.8
F32 = jnp.float32
BF16 = jnp.bfloat16
VSPEC = pl.BlockSpec(memory_space=pltpu.VMEM)


def shape_of(*dims, dtype=F32):
    return jax.ShapeDtypeStruct(dims, dtype)


FARSPEC = pl.BlockSpec(memory_space=pltpu.HBM)


def run_kernel(kernel, outs, args, scratch=(), aliases=None, flops=0, far=(), far_out=(), vmem=4):
    moved = sum(a.size * a.dtype.itemsize for a in args)
    return pl.pallas_call(
        kernel,
        out_shape=outs,
        in_specs=[FARSPEC if n in far else VSPEC for n in range(len(args))],
        out_specs=[FARSPEC if n in far_out else VSPEC for n in range(len(outs))],
        scratch_shapes=list(scratch),
        input_output_aliases=aliases or {},
        compiler_params=pltpu.CompilerParams(vmem_limit_bytes=int(vmem * 2**20)),
        cost_estimate=pl.CostEstimate(flops=flops, transcendentals=0, bytes_accessed=moved),
    )(*args)


def lane_index():
    return lax.broadcasted_iota(jnp.int32, (HALF, LANES), 1)


def row_index():
    return lax.broadcasted_iota(jnp.int32, (HALF, LANES), 0)


def spread(row):
    return jnp.broadcast_to(row, (HALF, LANES))


def pack_edges(packed, halves, j, lane):
    for half in range(2):
        m = 2 * j + half
        here = (lane >> 1) == m
        for c in range(COMPS):
            packed[c] = jnp.where(here, pltpu.roll(halves[c][half], 2 * m + 1, 1), packed[c])
    return packed


def part_faces(low_ref, high_ref, pair_ref, odd_ref):
    even = (lax.axis_index("wrap") & 1) == 0
    low, high = low_ref[:COMPS], high_ref[:COMPS]
    pair_ref[...] = jnp.where(even, high, low)
    odd_ref[...] = jnp.where(even, low, high)


def first_faces(start_ref, v_ref, slab_ref, pair_ref, odd_ref, edge_ref, low_ref, high_ref, sem):
    lane = lane_index()
    copy = pltpu.make_async_copy(start_ref, v_ref.at[:, :NJ], sem)
    copy.start()
    for c in range(COMPS):
        v_ref[c, NJ] = jnp.zeros((ROWS, LANES), F32)
    copy.wait()

    def step(j, packed):
        halves = [(v_ref[c, j, :HALF], v_ref[c, j, HALF:]) for c in range(COMPS)]
        for c in range(COMPS):
            low_ref[c, pl.ds(j, 1)] = halves[c][0][:1]
            high_ref[c, pl.ds(j, 1)] = halves[c][1][HALF - 1 :]
        return tuple(pack_edges(list(packed), halves, j, lane))

    packed = lax.fori_loop(
        0, NJ, step, tuple(jnp.zeros((HALF, LANES), F32) for _ in range(COMPS)), unroll=4
    )
    for c in range(COMPS):
        edge_ref[c] = packed[c]
        slab_ref[c] = v_ref[c, 0]
    part_faces(low_ref, high_ref, pair_ref, odd_ref)


def mirror_rows(slab_ref, pair_ref, odd_ref, out_ref):
    even = (lax.axis_index("wrap") & 1) == 0
    for c in range(COMPS):
        pair, odd = pair_ref[c, 0:1], odd_ref[c, 0:1]
        out_ref[c, 0:1] = jnp.where(even, pair, odd)
        for i in range(ROWS):
            out_ref[c, i + 1 : i + 2] = slab_ref[c, ROWS - 1 - i : ROWS - i]
        out_ref[c, ROWS + 1 : ROWS + 2] = jnp.where(even, odd, pair)
        out_ref[c, ROWS + 2 :] = jnp.zeros((24 - ROWS - 2, LANES), F32)


CHUNK = 4
CHUNKS = NJ // CHUNK
AHEAD = 3


def apply_blocks(stage, *refs):
    last = stage == 2
    *refs, even_stage_ref, odd_stage_ref = refs
    (v_ref, slab_ref, jac_ref, src_ref, dis_ref, near_ref, far_face_ref, pair_ref, odd_ref) = refs[:9]
    if stage == 0:
        out_ref, part_ref, low_ref, high_ref, edge_ref, wide_ref, base_ref = refs[9:16]
        q_ref, before_ref, after_ref, narrow_ref, sems = refs[16:]
    elif stage == 1:
        out_ref, part_ref, low_ref, high_ref, edge_ref, q_ref, before_ref, after_ref = refs[9:]
    else:
        far_ref, part_ref, final_ref, q_ref, before_ref, after_ref, out_ref, sems = refs[9:]

    def block_copy(n):
        at = pl.ds(n * CHUNK, CHUNK)
        return pltpu.make_async_copy(
            jac_ref.at[:, :, :, at], narrow_ref.at[:, :, :, at], sems.at[n]
        )

    def result_copy(n):
        at = pl.ds(n * CHUNK, CHUNK)
        return pltpu.make_async_copy(out_ref.at[:, at], far_ref.at[:, at], sems.at[n])

    if stage == 0:
        for n in range(AHEAD):
            block_copy(n).start()
    if last:
        final_copies = (
            pltpu.make_async_copy(v_ref.at[:, 1:NJ], final_ref.at[:, 1:], sems.at[CHUNKS]),
            pltpu.make_async_copy(slab_ref, final_ref.at[:, 0], sems.at[CHUNKS + 1]),
        )
        for copy in final_copies:
            copy.start()
    lane, row = lane_index(), row_index()
    place = lax.axis_index("span")
    has_down, has_up = place > 0, place < SPAN - 1
    swapped = (place & 1) == 1
    part_faces(far_face_ref, near_ref, after_ref, before_ref)
    even = (lane & 1) == 0
    for c in range(COMPS):
        up = jnp.where(swapped, odd_ref[c], pair_ref[c])
        down = jnp.where(swapped, pair_ref[c], odd_ref[c])
        from_up = jnp.where(has_up, pltpu.roll(up, LANES - 1, 1), 0.0)
        from_down = jnp.where(has_down, pltpu.roll(down, 1, 1), 0.0)
        q_ref[c] = jnp.where(even, from_up, from_down)
        if not last:
            out_ref[c, NJ] = jnp.zeros((ROWS, LANES), F32)
    first_lane, last_lane = lane == 0, lane == LANES - 1
    first_row, last_row = row == 0, row == HALF - 1

    def plane(c, j):
        if isinstance(j, int) and j < 0:
            return jnp.zeros((ROWS, LANES), F32)
        return slab_ref[c] if isinstance(j, int) and j == 0 else v_ref[c, j]

    def prepare(j, stage_ref):
        for c in range(COMPS):
            here = plane(c, j)
            a, b = here[:HALF], here[HALF:]
            before = spread(before_ref[c, pl.ds(j, 1)])
            after = spread(after_ref[c, pl.ds(j, 1)])
            a_up, b_up = pltpu.roll(a, HALF - 1, 0), pltpu.roll(b, HALF - 1, 0)
            a_dn, b_dn = pltpu.roll(a, 1, 0), pltpu.roll(b, 1, 0)
            next_i = (jnp.where(last_row, b_up, a_up), jnp.where(last_row, after, b_up))
            prev_i = (jnp.where(first_row, before, a_dn), jnp.where(first_row, a_dn, b_dn))
            for half, x in enumerate((a, b)):
                at = slice(half * HALF, (half + 1) * HALF)
                edge = pltpu.roll(q_ref[c], LANES - 1 - 4 * j - 2 * half, 1)
                next_k = jnp.where(last_lane, edge, pltpu.roll(x, LANES - 1, 1))
                prev_k = jnp.where(first_lane, edge, pltpu.roll(x, 1, 1))
                stage_ref[c, at] = next_i[half] - prev_i[half]
                stage_ref[COMPS + c, at] = next_k - prev_k
                stage_ref[2 * COMPS + c, at] = (next_i[half] + prev_i[half]) + (next_k + prev_k)

    def combine(j, stage_ref):
        total = [None] * COMPS
        sums = [None] * COMPS
        for b in range(COMPS):
            below = plane(b, j - 1)
            if last and isinstance(j, int) and j == NJ - 1:
                above = jnp.zeros((ROWS, LANES), F32)
            else:
                above = plane(b, j + 1)
            sums[b] = stage_ref[2 * COMPS + b] + (above + below)
            for d, diff in ((0, stage_ref[b]), (1, above - below), (2, stage_ref[COMPS + b])):
                for c in range(COMPS):
                    if stage == 0:
                        block = narrow_ref[d, c, b, j].astype(F32)
                        wide_ref[d, c, b, j] = block
                        if d == 1 and isinstance(j, int) and j == 0:
                            base_ref[c, b] = block
                    else:
                        block = jac_ref[d, c, b, j]
                    term = block * diff
                    total[c] = term if total[c] is None else total[c] + term
        dis = dis_ref[j]
        weight = None if last else (OMEGA / 6.0) / dis
        for c in range(COMPS):
            x = plane(c, j)
            rhs = src_ref[c, j] - total[c]
            if last:
                rest = rhs - dis * (6.0 * x - sums[c])
            else:
                rest = ((1.0 - OMEGA) * x + (OMEGA / 6.0) * sums[c]) + weight * rhs
            if isinstance(j, int) and j == 0:
                part_ref[c] = rest
            out_ref[c, j] = rest
            if not last:
                low_ref[c, pl.ds(j, 1)] = rest[:1]
                high_ref[c, pl.ds(j, 1)] = rest[ROWS - 1 :]

    def pack(j, packed):
        if last:
            return packed
        halves = [(out_ref[c, j, :HALF], out_ref[c, j, HALF:]) for c in range(COMPS)]
        return tuple(pack_edges(list(packed), halves, j, lane))

    def loop_step(t, packed):
        j = 2 * t + 2
        if stage == 0:

            @pl.when(j % CHUNK == 0)
            def _():
                n = j // CHUNK
                block_copy(n).wait()

                @pl.when(n + AHEAD < CHUNKS)
                def _():
                    block_copy(n + AHEAD).start()

        packed = pack(j - 1, packed)
        prepare(j + 1, odd_stage_ref)
        combine(j, even_stage_ref)
        packed = pack(j, packed)
        prepare(jnp.minimum(j + 2, NJ - 1), even_stage_ref)
        combine(j + 1, odd_stage_ref)
        if last:

            @pl.when(j % CHUNK == CHUNK - 2)
            def _():
                result_copy(j // CHUNK).start()

        return packed

    packed = () if last else tuple(jnp.zeros((HALF, LANES), F32) for _ in range(COMPS))
    if stage == 0:
        block_copy(0).wait()
        block_copy(AHEAD).start()
    prepare(0, even_stage_ref)
    prepare(1, odd_stage_ref)
    combine(0, even_stage_ref)
    packed = pack(0, packed)
    prepare(2, even_stage_ref)
    combine(1, odd_stage_ref)
    packed = lax.fori_loop(0, NJ // 2 - 1, loop_step, packed)
    packed = pack(NJ - 1, packed)
    if last:
        for n in range(CHUNKS):
            result_copy(n).wait()
        for copy in final_copies:
            copy.wait()
    else:
        for c in range(COMPS):
            edge_ref[c] = packed[c]


def add_ghosts(last, *refs):
    (slab_ref, base_ref, dis_ref, wall_ref, partner_ref, window_ref, part_ref) = refs[:7]
    if last:
        _, far_ref, out_ref, sem = refs[7:]
    else:
        low_in, high_in, edge_in, out_ref, pair_ref, odd_ref, edge_ref = refs[7:]
        part_faces(low_in, high_in, pair_ref, odd_ref)
        even = (lax.axis_index("wrap") & 1) == 0
    lane = lane_index()
    base = lax.axis_index("wrap") * ROWS
    row = lax.broadcasted_iota(jnp.int32, (ROWS, LANES), 0)
    shift = partner_ref[...] - (WRAP * ROWS - 1 - base - row)
    wall = wall_ref[...] == 1
    dis = dis_ref[0]
    ghosts = []
    for c in range(COMPS):
        rows = window_ref[c]
        lower, middle, upper = rows[:ROWS], rows[1 : ROWS + 1], rows[2 : ROWS + 2]
        chosen = jnp.where(shift == -1, upper, jnp.where(shift == 1, lower, middle))
        ghosts.append(jnp.where(wall, slab_ref[c], chosen))
    if not last:
        weight = (OMEGA / 6.0) / dis
    for c in range(COMPS):
        total = base_ref[c, 0] * ghosts[0]
        for b in range(1, COMPS):
            total = total + base_ref[c, b] * ghosts[b]
        if last:
            fresh = part_ref[c] + (dis * ghosts[c] + total)
        else:
            fresh = part_ref[c] + ((OMEGA / 6.0) * ghosts[c] + weight * total)
        out_ref[c] = fresh
        if not last:
            low, high = fresh[:1], fresh[ROWS - 1 :]
            pair_ref[c, 0:1] = jnp.where(even, high, low)
            odd_ref[c, 0:1] = jnp.where(even, low, high)
            edge = jnp.where(lane < 2, pltpu.roll(fresh[:HALF], 1, 1), edge_in[c])
            here = (lane == 2) | (lane == 3)
            edge_ref[c] = jnp.where(here, pltpu.roll(fresh[HALF:], 3, 1), edge)
    if last:
        copy = pltpu.make_async_copy(out_ref, far_ref.at[:, 0], sem)
        copy.start()
        copy.wait()


POINT_LANES = 64


def surface_sums(*refs):
    slab_ref, slope_ref, wall_ref, points_ref, weights_ref, face_ref = refs[:6]
    kept_ref, bundle_ref, left_ref, right_ref, sum_ref = refs[6:]
    bundle_ref[:COMPS] = face_ref[...]
    wall = wall_ref[...].astype(F32)
    grads = []
    for x in range(3):
        total = slope_ref[x, 0] * slab_ref[0]
        for a in range(1, COMPS):
            total = total + slope_ref[x, a] * slab_ref[a]
        grads.append(total * wall)
    owner = lax.broadcasted_iota(jnp.int32, (WRAP, LANES), 0)
    inner = lax.broadcasted_iota(jnp.int32, (POINT_LANES, LANES), 0)
    for slot in range(LISTS):
        points = points_ref[slot]
        scale = weights_ref[slot]
        major, minor = points >> 6, points & (POINT_LANES - 1)
        parts = []
        for x in range(3):
            value = grads[x] * scale
            high = value.astype(BF16).astype(F32)
            parts.append((high, value - high))
        for i in range(ROWS):
            at = pl.ds((slot * ROWS + i) * LANES, LANES)
            mine = owner == jnp.broadcast_to(major[i : i + 1], (WRAP, LANES))
            for x in range(3):
                for part in range(2):
                    value = jnp.broadcast_to(parts[x][part][i : i + 1], (WRAP, LANES))
                    left_ref[x * 2 + part, :, at] = jnp.where(mine, value, 0.0).astype(BF16)
            same = inner == jnp.broadcast_to(minor[i : i + 1], (POINT_LANES, LANES))
            right_ref[:, at] = jnp.where(same, 1.0, 0.0).astype(BF16)
    left = left_ref[...].reshape(6 * WRAP, LISTS * ROWS * LANES)
    product = lax.dot_general(
        left, right_ref[...], (((1,), (1,)), ((), ())), preferred_element_type=F32
    )
    sum_ref[...] = jnp.zeros_like(sum_ref)
    for x in range(3):
        first = product[2 * x * WRAP : (2 * x + 1) * WRAP]
        second = product[(2 * x + 1) * WRAP : (2 * x + 2) * WRAP]
        both = first + second
        for w in range(WRAP):
            place = (w & 9) | ((w ^ (w >> 1)) & 2) | (w & 4)
            sum_ref[place, x : x + 1, :POINT_LANES] = both[w : w + 1]
    mine = lax.axis_index("wrap") & 1
    for n in range(WRAP // 2):
        kept_ref[n] = sum_ref[2 * n + mine]
        bundle_ref[COMPS + n // 4, pl.ds(n % 4 * HALF, HALF)] = sum_ref[2 * n + 1 - mine]


def halve_bundle(kept_in, bundle_ref, kept_ref, sent_ref, sum_ref):
    for n in range(WRAP // 2):
        sum_ref[n] = kept_in[n] + bundle_ref[COMPS + n // 4, n % 4 * HALF : (n % 4 + 1) * HALF]
    w = lax.axis_index("wrap")
    deal(((w >> 1) ^ (w >> 2)) & 1, sum_ref, kept_ref, sent_ref)


def halve(kept_in, got_ref, kept_ref, sent_ref, sum_ref):
    sum_ref[...] = kept_in[...] + got_ref[...]
    deal((lax.axis_index("wrap") >> 2) & 1, sum_ref, kept_ref, sent_ref)


def deal(mine, sum_ref, kept_ref, sent_ref):
    for n in range(kept_ref.shape[0]):
        kept_ref[n] = sum_ref[2 * n + mine]
        sent_ref[n] = sum_ref[2 * n + 1 - mine]


def halve_lanes(kept_in, got_ref, kept_ref, sent_ref):
    first, second = kept_in[0] + got_ref[0], kept_in[1] + got_ref[1]
    mine = (lax.axis_index("wrap") >> 3) ^ (lax.axis_index("span") & 1)
    odd = (lane_index() >> 3) & 1
    take = odd == mine
    kept_ref[0] = jnp.where(take, first, second)
    sent_ref[0] = jnp.where(take, second, first)


def add_tiles(a_ref, b_ref, out_ref):
    out_ref[...] = a_ref[...] + b_ref[...]


def finish_points(a_ref, b_ref, out_ref):
    total = a_ref[0] + b_ref[0]
    out_ref[...] = pltpu.roll(total, LANES - 8 * lax.axis_index("span"), 1)[:3, :8]


def masked(wrap_mask, span_mask):
    return [
        (w * SPAN + s, (w ^ wrap_mask) * SPAN + (s ^ span_mask))
        for w in range(WRAP)
        for s in range(SPAN)
    ]


FOLDS = (masked(2, 0), masked(6, 0), masked(8, 0), masked(8, 1), masked(0, 2), masked(0, 6))


def fold(x, n):
    return lax.ppermute(x, ("wrap", "span"), FOLDS[n - 1])


def reduce_points(kept, bundle):
    tiles = lambda n: [shape_of(n, HALF, LANES)]
    room = lambda n: (pltpu.VMEM((n, HALF, LANES), F32),)
    kept, sent = run_kernel(halve_bundle, tiles(4) * 2, (kept, bundle), scratch=room(8))
    args = (kept, fold(sent, 1))
    kept, sent = run_kernel(halve, tiles(2) * 2, args, scratch=room(4))
    args = (kept, fold(sent, 2))
    kept, sent = run_kernel(halve_lanes, tiles(1) * 2, args)
    got = fold(sent, 3)
    for n in range(4, 7):
        (kept,) = run_kernel(add_tiles, tiles(1), (kept, got))
        got = fold(kept, n)
    (out,) = run_kernel(finish_points, [shape_of(3, 8)], (kept, got))
    return out


WRAP_PAIR = [(i, i ^ 1) for i in range(WRAP)]
WRAP_ODD = [(i, (i + 1) % WRAP if i % 2 else (i - 1) % WRAP) for i in range(WRAP)]
SPAN_PAIR = [(i, i ^ 1) for i in range(SPAN)]
SPAN_ODD = [(i, (i + 1) % SPAN if i % 2 else (i - 1) % SPAN) for i in range(SPAN)]
MIRROR = [(i, WRAP - 1 - i) for i in range(WRAP)]

FIELD = (COMPS, NJ, ROWS, LANES)
TALL = (COMPS, NJ + 1, ROWS, LANES)
SLAB = (COMPS, ROWS, LANES)
STAGE = (3 * COMPS, ROWS, LANES)
FACE = (COMPS, NJ, LANES)
EDGE = (COMPS, HALF, LANES)
BLOCKS = (3, COMPS, COMPS, NJ, ROWS, LANES)
SWEEP_FLOPS = 160 * COMPS * NJ * ROWS * LANES
DMA = pltpu.SemaphoreType.DMA


def exchange(slab, pair_face, odd_face, edge):
    near = lax.ppermute(pair_face, "wrap", WRAP_PAIR)
    far = lax.ppermute(odd_face, "wrap", WRAP_ODD)
    odd = lax.ppermute(edge, "span", SPAN_ODD)
    pair = lax.ppermute(edge, "span", SPAN_PAIR)
    (rows,) = run_kernel(mirror_rows, [shape_of(COMPS, 24, LANES)], (slab, near, far))
    window = lax.ppermute(rows, "wrap", MIRROR)
    return (near, far, pair, odd), window


def operator_step(stage, v, slab, faces, blocks, base, fixed):
    source, dissipation, wall, partner = fixed
    halos, window = exchange(slab, *faces)
    args = (v, slab, blocks, source, dissipation, *halos)
    kernel = functools.partial(apply_blocks, stage)
    if stage < 2:
        outs = [shape_of(*d) for d in (TALL, SLAB, FACE, FACE, EDGE)]
        scratch = [pltpu.VMEM(EDGE, F32), pltpu.VMEM(FACE, F32), pltpu.VMEM(FACE, F32)]
        if stage == 0:
            outs += [shape_of(*BLOCKS), shape_of(*BLOCKS[1:3], ROWS, LANES)]
            scratch += [pltpu.VMEM(BLOCKS, BF16), DMA((CHUNKS,))]
        scratch += [pltpu.VMEM(STAGE, F32)] * 2
        v, part, *rest = run_kernel(
            kernel,
            outs,
            args,
            scratch=scratch,
            flops=SWEEP_FLOPS,
            far=(2,) if stage == 0 else (),
            vmem=12 if stage == 0 else 4,
        )
        if stage == 0:
            *rest, blocks, base = rest
        slab, *faces = run_kernel(
            functools.partial(add_ghosts, False),
            [shape_of(*d) for d in (SLAB, FACE, FACE, EDGE)],
            (slab, base, dissipation, wall, partner, window, part, *rest),
            flops=1000000,
        )
        return v, slab, faces, blocks, base
    residual, part, final = run_kernel(
        kernel,
        [shape_of(*FIELD), shape_of(*SLAB), shape_of(*FIELD)],
        args,
        scratch=(
            pltpu.VMEM(EDGE, F32),
            pltpu.VMEM(FACE, F32),
            pltpu.VMEM(FACE, F32),
            pltpu.VMEM(FIELD, F32),
            DMA((CHUNKS + 2,)),
            pltpu.VMEM(STAGE, F32),
            pltpu.VMEM(STAGE, F32),
        ),
        flops=SWEEP_FLOPS,
        far_out=(0, 2),
    )
    (residual,) = run_kernel(
        functools.partial(add_ghosts, True),
        [shape_of(*FIELD)],
        (slab, base, dissipation, wall, partner, window, part, residual),
        scratch=(pltpu.VMEM(SLAB, F32), DMA),
        aliases={7: 0},
        flops=1000000,
        far=(7,),
        far_out=(0,),
    )
    return final, residual, halos[0]


def program(
    adjoint_start,
    adjoint_source,
    jacobians,
    dissipation,
    wall_mask,
    wake_partner,
    surface_slopes,
    control_points,
    control_weights,
):
    fixed = (adjoint_source, dissipation, wall_mask, wake_partner)
    v, slab, *faces = run_kernel(
        first_faces,
        [shape_of(*d) for d in (TALL, SLAB, FACE, FACE, EDGE)],
        (pltpu.with_memory_space_constraint(adjoint_start, pltpu.HBM),),
        scratch=(pltpu.VMEM(FACE, F32), pltpu.VMEM(FACE, F32), DMA),
        flops=1000000,
        far=(0,),
    )
    blocks, base = pltpu.with_memory_space_constraint(jacobians, pltpu.HBM), None
    for stage in range(2):
        v, slab, faces, blocks, base = operator_step(
            stage, v, slab, faces, blocks, base, fixed
        )
    kept, bundle = run_kernel(
        surface_sums,
        [shape_of(WRAP // 2, HALF, LANES), shape_of(COMPS + 2, NJ, LANES)],
        (slab, surface_slopes, wall_mask, control_points, control_weights, faces[0]),
        scratch=(
            pltpu.VMEM((6, WRAP, LISTS * ROWS * LANES), BF16),
            pltpu.VMEM((POINT_LANES, LISTS * ROWS * LANES), BF16),
            pltpu.VMEM((WRAP, HALF, LANES), F32),
        ),
        flops=10000000,
        vmem=8,
    )
    faces[0] = bundle
    final, residual, bundle = operator_step(2, v, slab, faces, blocks, base, fixed)
    shape_gradient = reduce_points(kept, bundle)
    return final, residual, shape_gradient


def solution(mesh):
    in_specs = (
        P(None, None, "wrap", "span"),
        P(None, None, "wrap", "span"),
        P(None, None, None, None, "wrap", "span"),
        P(None, "wrap", "span"),
        P("wrap", "span"),
        P("wrap", "span"),
        P(None, None, "wrap", "span"),
        P(None, "wrap", "span"),
        P(None, "wrap", "span"),
    )
    out_specs = (
        P(None, None, "wrap", "span"),
        P(None, None, "wrap", "span"),
        P(None, ("wrap", "span")),
    )
    return jax.shard_map(program, mesh=mesh, in_specs=in_specs, out_specs=out_specs, check_vma=False)
```

```python
import functools

import jax
import jax.numpy as jnp
from jax import lax
from jax.experimental import pallas as pl
from jax.experimental.pallas import tpu as pltpu
from jax.sharding import PartitionSpec as P

COMPS = 5
NJ = 32
ROWS = 16
LANES = 128
HALF = 8
WRAP = 16
SPAN = 8
LISTS = 4
OMEGA = 0.8
F32 = jnp.float32
BF16 = jnp.bfloat16
VSPEC = pl.BlockSpec(memory_space=pltpu.VMEM)


def shape_of(*dims, dtype=F32):
    return jax.ShapeDtypeStruct(dims, dtype)


FARSPEC = pl.BlockSpec(memory_space=pltpu.HBM)


def run_kernel(kernel, outs, args, scratch=(), aliases=None, flops=0, far=(), far_out=(), vmem=4):
    moved = sum(a.size * a.dtype.itemsize for a in args)
    return pl.pallas_call(
        kernel,
        out_shape=outs,
        in_specs=[FARSPEC if n in far else VSPEC for n in range(len(args))],
        out_specs=[FARSPEC if n in far_out else VSPEC for n in range(len(outs))],
        scratch_shapes=list(scratch),
        input_output_aliases=aliases or {},
        compiler_params=pltpu.CompilerParams(vmem_limit_bytes=int(vmem * 2**20)),
        cost_estimate=pl.CostEstimate(flops=flops, transcendentals=0, bytes_accessed=moved),
    )(*args)


def lane_index():
    return lax.broadcasted_iota(jnp.int32, (HALF, LANES), 1)


def row_index():
    return lax.broadcasted_iota(jnp.int32, (HALF, LANES), 0)


def spread(row):
    return jnp.broadcast_to(row, (HALF, LANES))


def pack_edges(packed, halves, j, lane):
    for half in range(2):
        m = 2 * j + half
        here = (lane >> 1) == m
        for c in range(COMPS):
            packed[c] = jnp.where(here, pltpu.roll(halves[c][half], 2 * m + 1, 1), packed[c])
    return packed


def part_faces(low_ref, high_ref, pair_ref, odd_ref):
    even = (lax.axis_index("wrap") & 1) == 0
    low, high = low_ref[:COMPS], high_ref[:COMPS]
    pair_ref[...] = jnp.where(even, high, low)
    odd_ref[...] = jnp.where(even, low, high)


def first_faces(start_ref, v_ref, slab_ref, pair_ref, odd_ref, edge_ref, low_ref, high_ref, sem):
    lane = lane_index()
    copies = []
    for n in range(4):
        at = pl.ds(n * 8, 8)
        copies.append(pltpu.make_async_copy(start_ref.at[:, at], v_ref.at[:, at], sem.at[n]))
        copies[-1].start()
    for c in range(COMPS):
        v_ref[c, NJ] = jnp.zeros((ROWS, LANES), F32)

    def step(j, packed):
        halves = [(v_ref[c, j, :HALF], v_ref[c, j, HALF:]) for c in range(COMPS)]
        for c in range(COMPS):
            low_ref[c, pl.ds(j, 1)] = halves[c][0][:1]
            high_ref[c, pl.ds(j, 1)] = halves[c][1][HALF - 1 :]
        return tuple(pack_edges(list(packed), halves, j, lane))

    packed = tuple(jnp.zeros((HALF, LANES), F32) for _ in range(COMPS))
    for n in range(4):
        copies[n].wait()
        packed = lax.fori_loop(n * 8, n * 8 + 8, step, packed, unroll=8)
    for c in range(COMPS):
        edge_ref[c] = packed[c]
        slab_ref[c] = v_ref[c, 0]
    part_faces(low_ref, high_ref, pair_ref, odd_ref)


def mirror_rows(slab_ref, pair_ref, odd_ref, out_ref):
    even = (lax.axis_index("wrap") & 1) == 0
    for c in range(COMPS):
        pair, odd = pair_ref[c, 0:1], odd_ref[c, 0:1]
        out_ref[c, 0:1] = jnp.where(even, pair, odd)
        for i in range(ROWS):
            out_ref[c, i + 1 : i + 2] = slab_ref[c, ROWS - 1 - i : ROWS - i]
        out_ref[c, ROWS + 1 : ROWS + 2] = jnp.where(even, odd, pair)
        out_ref[c, ROWS + 2 :] = jnp.zeros((24 - ROWS - 2, LANES), F32)


CHUNK = 4
CHUNKS = NJ // CHUNK
AHEAD = 3


def apply_blocks(stage, *refs):
    last = stage == 2
    *refs, even_stage_ref, odd_stage_ref = refs
    (v_ref, slab_ref, jac_ref, src_ref, dis_ref, near_ref, far_face_ref, pair_ref, odd_ref) = refs[:9]
    if stage == 0:
        out_ref, part_ref, low_ref, high_ref, edge_ref, wide_ref, base_ref = refs[9:16]
        q_ref, before_ref, after_ref, narrow_ref, sems = refs[16:]
    elif stage == 1:
        out_ref, part_ref, low_ref, high_ref, edge_ref, q_ref, before_ref, after_ref = refs[9:]
    else:
        far_ref, part_ref, final_ref, q_ref, before_ref, after_ref, out_ref, sems = refs[9:]

    def block_copy(n):
        at = pl.ds(n * CHUNK, CHUNK)
        return pltpu.make_async_copy(
            jac_ref.at[:, :, :, at], narrow_ref.at[:, :, :, at], sems.at[n]
        )

    def result_copy(n):
        at = pl.ds(n * CHUNK, CHUNK)
        return pltpu.make_async_copy(out_ref.at[:, at], far_ref.at[:, at], sems.at[n])

    if stage == 0:
        for n in range(AHEAD):
            block_copy(n).start()
    if last:
        final_copies = (
            pltpu.make_async_copy(v_ref.at[:, 1:NJ], final_ref.at[:, 1:], sems.at[CHUNKS]),
            pltpu.make_async_copy(slab_ref, final_ref.at[:, 0], sems.at[CHUNKS + 1]),
        )
        for copy in final_copies:
            copy.start()
    lane, row = lane_index(), row_index()
    place = lax.axis_index("span")
    has_down, has_up = place > 0, place < SPAN - 1
    swapped = (place & 1) == 1
    part_faces(far_face_ref, near_ref, after_ref, before_ref)
    even = (lane & 1) == 0
    for c in range(COMPS):
        up = jnp.where(swapped, odd_ref[c], pair_ref[c])
        down = jnp.where(swapped, pair_ref[c], odd_ref[c])
        from_up = jnp.where(has_up, pltpu.roll(up, LANES - 1, 1), 0.0)
        from_down = jnp.where(has_down, pltpu.roll(down, 1, 1), 0.0)
        q_ref[c] = jnp.where(even, from_up, from_down)
        if not last:
            out_ref[c, NJ] = jnp.zeros((ROWS, LANES), F32)
    first_lane, last_lane = lane == 0, lane == LANES - 1
    first_row, last_row = row == 0, row == HALF - 1

    def plane(c, j):
        if isinstance(j, int) and j < 0:
            return jnp.zeros((ROWS, LANES), F32)
        return slab_ref[c] if isinstance(j, int) and j == 0 else v_ref[c, j]

    def prepare(j, stage_ref):
        for c in range(COMPS):
            here = plane(c, j)
            a, b = here[:HALF], here[HALF:]
            before = spread(before_ref[c, pl.ds(j, 1)])
            after = spread(after_ref[c, pl.ds(j, 1)])
            a_up, b_up = pltpu.roll(a, HALF - 1, 0), pltpu.roll(b, HALF - 1, 0)
            a_dn, b_dn = pltpu.roll(a, 1, 0), pltpu.roll(b, 1, 0)
            next_i = (jnp.where(last_row, b_up, a_up), jnp.where(last_row, after, b_up))
            prev_i = (jnp.where(first_row, before, a_dn), jnp.where(first_row, a_dn, b_dn))
            for half, x in enumerate((a, b)):
                at = slice(half * HALF, (half + 1) * HALF)
                edge = pltpu.roll(q_ref[c], LANES - 1 - 4 * j - 2 * half, 1)
                next_k = jnp.where(last_lane, edge, pltpu.roll(x, LANES - 1, 1))
                prev_k = jnp.where(first_lane, edge, pltpu.roll(x, 1, 1))
                stage_ref[c, at] = next_i[half] - prev_i[half]
                stage_ref[COMPS + c, at] = next_k - prev_k
                stage_ref[2 * COMPS + c, at] = (next_i[half] + prev_i[half]) + (next_k + prev_k)

    def combine(j, stage_ref):
        total = [None] * COMPS
        sums = [None] * COMPS
        for b in range(COMPS):
            below = plane(b, j - 1)
            if last and isinstance(j, int) and j == NJ - 1:
                above = jnp.zeros((ROWS, LANES), F32)
            else:
                above = plane(b, j + 1)
            sums[b] = stage_ref[2 * COMPS + b] + (above + below)
            for d, diff in ((0, stage_ref[b]), (1, above - below), (2, stage_ref[COMPS + b])):
                for c in range(COMPS):
                    if stage == 0:
                        block = narrow_ref[d, c, b, j].astype(F32)
                        wide_ref[d, c, b, j] = block
                        if d == 1 and isinstance(j, int) and j == 0:
                            base_ref[c, b] = block
                    else:
                        block = jac_ref[d, c, b, j]
                    term = block * diff
                    total[c] = term if total[c] is None else total[c] + term
        dis = dis_ref[j]
        weight = None if last else (OMEGA / 6.0) / dis
        for c in range(COMPS):
            x = plane(c, j)
            rhs = src_ref[c, j] - total[c]
            if last:
                rest = rhs - dis * (6.0 * x - sums[c])
            else:
                rest = ((1.0 - OMEGA) * x + (OMEGA / 6.0) * sums[c]) + weight * rhs
            if isinstance(j, int) and j == 0:
                part_ref[c] = rest
            out_ref[c, j] = rest
            if not last:
                low_ref[c, pl.ds(j, 1)] = rest[:1]
                high_ref[c, pl.ds(j, 1)] = rest[ROWS - 1 :]

    def pack(j, packed):
        if last:
            return packed
        halves = [(out_ref[c, j, :HALF], out_ref[c, j, HALF:]) for c in range(COMPS)]
        return tuple(pack_edges(list(packed), halves, j, lane))

    def loop_step(t, packed):
        j = 2 * t + 2
        if stage == 0:

            @pl.when(j % CHUNK == 0)
            def _():
                n = j // CHUNK
                block_copy(n).wait()

                @pl.when(n + AHEAD < CHUNKS)
                def _():
                    block_copy(n + AHEAD).start()

        packed = pack(j - 1, packed)
        prepare(j + 1, odd_stage_ref)
        combine(j, even_stage_ref)
        packed = pack(j, packed)
        prepare(jnp.minimum(j + 2, NJ - 1), even_stage_ref)
        combine(j + 1, odd_stage_ref)
        if last:

            @pl.when(j % CHUNK == CHUNK - 2)
            def _():
                result_copy(j // CHUNK).start()

        return packed

    packed = () if last else tuple(jnp.zeros((HALF, LANES), F32) for _ in range(COMPS))
    if stage == 0:
        block_copy(0).wait()
        block_copy(AHEAD).start()
    prepare(0, even_stage_ref)
    prepare(1, odd_stage_ref)
    combine(0, even_stage_ref)
    packed = pack(0, packed)
    prepare(2, even_stage_ref)
    combine(1, odd_stage_ref)
    packed = lax.fori_loop(0, NJ // 2 - 1, loop_step, packed)
    packed = pack(NJ - 1, packed)
    if last:
        for n in range(CHUNKS):
            result_copy(n).wait()
        for copy in final_copies:
            copy.wait()
    else:
        for c in range(COMPS):
            edge_ref[c] = packed[c]


def add_ghosts(last, *refs):
    (slab_ref, base_ref, dis_ref, wall_ref, partner_ref, window_ref, part_ref) = refs[:7]
    if last:
        _, far_ref, out_ref, sem = refs[7:]
    else:
        low_in, high_in, edge_in, out_ref, pair_ref, odd_ref, edge_ref = refs[7:]
        part_faces(low_in, high_in, pair_ref, odd_ref)
        even = (lax.axis_index("wrap") & 1) == 0
    lane = lane_index()
    base = lax.axis_index("wrap") * ROWS
    row = lax.broadcasted_iota(jnp.int32, (ROWS, LANES), 0)
    shift = partner_ref[...] - (WRAP * ROWS - 1 - base - row)
    wall = wall_ref[...] == 1
    dis = dis_ref[0]
    ghosts = []
    for c in range(COMPS):
        rows = window_ref[c]
        lower, middle, upper = rows[:ROWS], rows[1 : ROWS + 1], rows[2 : ROWS + 2]
        chosen = jnp.where(shift == -1, upper, jnp.where(shift == 1, lower, middle))
        ghosts.append(jnp.where(wall, slab_ref[c], chosen))
    if not last:
        weight = (OMEGA / 6.0) / dis
    for c in range(COMPS):
        total = base_ref[c, 0] * ghosts[0]
        for b in range(1, COMPS):
            total = total + base_ref[c, b] * ghosts[b]
        if last:
            fresh = part_ref[c] + (dis * ghosts[c] + total)
        else:
            fresh = part_ref[c] + ((OMEGA / 6.0) * ghosts[c] + weight * total)
        out_ref[c] = fresh
        if not last:
            low, high = fresh[:1], fresh[ROWS - 1 :]
            pair_ref[c, 0:1] = jnp.where(even, high, low)
            odd_ref[c, 0:1] = jnp.where(even, low, high)
            edge = jnp.where(lane < 2, pltpu.roll(fresh[:HALF], 1, 1), edge_in[c])
            here = (lane == 2) | (lane == 3)
            edge_ref[c] = jnp.where(here, pltpu.roll(fresh[HALF:], 3, 1), edge)
    if last:
        copy = pltpu.make_async_copy(out_ref, far_ref.at[:, 0], sem)
        copy.start()
        copy.wait()


POINT_LANES = 64


def surface_sums(*refs):
    slab_ref, slope_ref, wall_ref, points_ref, weights_ref, face_ref = refs[:6]
    kept_ref, bundle_ref, left_ref, right_ref, sum_ref = refs[6:]
    bundle_ref[:COMPS] = face_ref[...]
    wall = wall_ref[...].astype(F32)
    grads = []
    for x in range(3):
        total = slope_ref[x, 0] * slab_ref[0]
        for a in range(1, COMPS):
            total = total + slope_ref[x, a] * slab_ref[a]
        grads.append(total * wall)
    owner = lax.broadcasted_iota(jnp.int32, (WRAP, LANES), 0)
    inner = lax.broadcasted_iota(jnp.int32, (POINT_LANES, LANES), 0)
    for slot in range(LISTS):
        points = points_ref[slot]
        scale = weights_ref[slot]
        major, minor = points >> 6, points & (POINT_LANES - 1)
        parts = []
        for x in range(3):
            value = grads[x] * scale
            high = value.astype(BF16).astype(F32)
            parts.append((high, value - high))
        for i in range(ROWS):
            at = pl.ds((slot * ROWS + i) * LANES, LANES)
            mine = owner == jnp.broadcast_to(major[i : i + 1], (WRAP, LANES))
            for x in range(3):
                for part in range(2):
                    value = jnp.broadcast_to(parts[x][part][i : i + 1], (WRAP, LANES))
                    left_ref[x * 2 + part, :, at] = jnp.where(mine, value, 0.0).astype(BF16)
            same = inner == jnp.broadcast_to(minor[i : i + 1], (POINT_LANES, LANES))
            right_ref[:, at] = jnp.where(same, 1.0, 0.0).astype(BF16)
    left = left_ref[...].reshape(6 * WRAP, LISTS * ROWS * LANES)
    product = lax.dot_general(
        left, right_ref[...], (((1,), (1,)), ((), ())), preferred_element_type=F32
    )
    sum_ref[...] = jnp.zeros_like(sum_ref)
    for x in range(3):
        first = product[2 * x * WRAP : (2 * x + 1) * WRAP]
        second = product[(2 * x + 1) * WRAP : (2 * x + 2) * WRAP]
        both = first + second
        for w in range(WRAP):
            place = (w & 9) | ((w ^ (w >> 1)) & 2) | (w & 4)
            sum_ref[place, x : x + 1, :POINT_LANES] = both[w : w + 1]
    mine = lax.axis_index("wrap") & 1
    for n in range(WRAP // 2):
        kept_ref[n] = sum_ref[2 * n + mine]
        bundle_ref[COMPS + n // 4, pl.ds(n % 4 * HALF, HALF)] = sum_ref[2 * n + 1 - mine]


def halve_bundle(kept_in, bundle_ref, kept_ref, sent_ref, sum_ref):
    for n in range(WRAP // 2):
        sum_ref[n] = kept_in[n] + bundle_ref[COMPS + n // 4, n % 4 * HALF : (n % 4 + 1) * HALF]
    w = lax.axis_index("wrap")
    deal(((w >> 1) ^ (w >> 2)) & 1, sum_ref, kept_ref, sent_ref)


def halve(kept_in, got_ref, kept_ref, sent_ref, sum_ref):
    sum_ref[...] = kept_in[...] + got_ref[...]
    deal((lax.axis_index("wrap") >> 2) & 1, sum_ref, kept_ref, sent_ref)


def deal(mine, sum_ref, kept_ref, sent_ref):
    for n in range(kept_ref.shape[0]):
        kept_ref[n] = sum_ref[2 * n + mine]
        sent_ref[n] = sum_ref[2 * n + 1 - mine]


def halve_lanes(kept_in, got_ref, kept_ref, sent_ref):
    first, second = kept_in[0] + got_ref[0], kept_in[1] + got_ref[1]
    mine = (lax.axis_index("wrap") >> 3) ^ (lax.axis_index("span") & 1)
    odd = (lane_index() >> 3) & 1
    take = odd == mine
    kept_ref[0] = jnp.where(take, first, second)
    sent_ref[0] = jnp.where(take, second, first)


def add_tiles(a_ref, b_ref, out_ref):
    out_ref[...] = a_ref[...] + b_ref[...]


def finish_points(a_ref, b_ref, c_ref, d_ref, out_ref):
    total = (a_ref[0] + b_ref[0]) + (c_ref[0] + d_ref[0])
    out_ref[...] = pltpu.roll(total, LANES - 8 * lax.axis_index("span"), 1)[:3, :8]


def masked(wrap_mask, span_mask):
    return [
        (w * SPAN + s, (w ^ wrap_mask) * SPAN + (s ^ span_mask))
        for w in range(WRAP)
        for s in range(SPAN)
    ]


FOLDS = (masked(2, 0), masked(6, 0), masked(8, 0), masked(8, 1), masked(0, 2), masked(0, 6), masked(0, 4))


def fold(x, n):
    return lax.ppermute(x, ("wrap", "span"), FOLDS[n - 1])


def reduce_points(kept, bundle):
    tiles = lambda n: [shape_of(n, HALF, LANES)]
    room = lambda n: (pltpu.VMEM((n, HALF, LANES), F32),)
    kept, sent = run_kernel(halve_bundle, tiles(4) * 2, (kept, bundle), scratch=room(8))
    args = (kept, fold(sent, 1))
    kept, sent = run_kernel(halve, tiles(2) * 2, args, scratch=room(4))
    args = (kept, fold(sent, 2))
    kept, sent = run_kernel(halve_lanes, tiles(1) * 2, args)
    got = fold(sent, 3)
    (kept,) = run_kernel(add_tiles, tiles(1), (kept, got))
    got = fold(kept, 4)
    (kept,) = run_kernel(add_tiles, tiles(1), (kept, got))
    others = [fold(kept, n) for n in (5, 6, 7)]
    (out,) = run_kernel(finish_points, [shape_of(3, 8)], (kept, *others))
    return out


WRAP_PAIR = [(i, i ^ 1) for i in range(WRAP)]
WRAP_ODD = [(i, (i + 1) % WRAP if i % 2 else (i - 1) % WRAP) for i in range(WRAP)]
SPAN_PAIR = [(i, i ^ 1) for i in range(SPAN)]
SPAN_ODD = [(i, (i + 1) % SPAN if i % 2 else (i - 1) % SPAN) for i in range(SPAN)]
MIRROR = [(i, WRAP - 1 - i) for i in range(WRAP)]

FIELD = (COMPS, NJ, ROWS, LANES)
TALL = (COMPS, NJ + 1, ROWS, LANES)
SLAB = (COMPS, ROWS, LANES)
STAGE = (3 * COMPS, ROWS, LANES)
FACE = (COMPS, NJ, LANES)
EDGE = (COMPS, HALF, LANES)
BLOCKS = (3, COMPS, COMPS, NJ, ROWS, LANES)
SWEEP_FLOPS = 160 * COMPS * NJ * ROWS * LANES
DMA = pltpu.SemaphoreType.DMA


def exchange(slab, pair_face, odd_face, edge):
    near = lax.ppermute(pair_face, "wrap", WRAP_PAIR)
    far = lax.ppermute(odd_face, "wrap", WRAP_ODD)
    odd = lax.ppermute(edge, "span", SPAN_ODD)
    pair = lax.ppermute(edge, "span", SPAN_PAIR)
    (rows,) = run_kernel(mirror_rows, [shape_of(COMPS, 24, LANES)], (slab, near, far))
    window = lax.ppermute(rows, "wrap", MIRROR)
    return (near, far, pair, odd), window


def operator_step(stage, v, slab, faces, blocks, base, fixed):
    source, dissipation, wall, partner = fixed
    halos, window = exchange(slab, *faces)
    args = (v, slab, blocks, source, dissipation, *halos)
    kernel = functools.partial(apply_blocks, stage)
    if stage < 2:
        outs = [shape_of(*d) for d in (TALL, SLAB, FACE, FACE, EDGE)]
        scratch = [pltpu.VMEM(EDGE, F32), pltpu.VMEM(FACE, F32), pltpu.VMEM(FACE, F32)]
        if stage == 0:
            outs += [shape_of(*BLOCKS), shape_of(*BLOCKS[1:3], ROWS, LANES)]
            scratch += [pltpu.VMEM(BLOCKS, BF16), DMA((CHUNKS,))]
        scratch += [pltpu.VMEM(STAGE, F32)] * 2
        v, part, *rest = run_kernel(
            kernel,
            outs,
            args,
            scratch=scratch,
            flops=SWEEP_FLOPS,
            far=(2,) if stage == 0 else (),
            vmem=12 if stage == 0 else 4,
        )
        if stage == 0:
            *rest, blocks, base = rest
        slab, *faces = run_kernel(
            functools.partial(add_ghosts, False),
            [shape_of(*d) for d in (SLAB, FACE, FACE, EDGE)],
            (slab, base, dissipation, wall, partner, window, part, *rest),
            flops=1000000,
        )
        return v, slab, faces, blocks, base
    residual, part, final = run_kernel(
        kernel,
        [shape_of(*FIELD), shape_of(*SLAB), shape_of(*FIELD)],
        args,
        scratch=(
            pltpu.VMEM(EDGE, F32),
            pltpu.VMEM(FACE, F32),
            pltpu.VMEM(FACE, F32),
            pltpu.VMEM(FIELD, F32),
            DMA((CHUNKS + 2,)),
            pltpu.VMEM(STAGE, F32),
            pltpu.VMEM(STAGE, F32),
        ),
        flops=SWEEP_FLOPS,
        far_out=(0, 2),
    )
    (residual,) = run_kernel(
        functools.partial(add_ghosts, True),
        [shape_of(*FIELD)],
        (slab, base, dissipation, wall, partner, window, part, residual),
        scratch=(pltpu.VMEM(SLAB, F32), DMA),
        aliases={7: 0},
        flops=1000000,
        far=(7,),
        far_out=(0,),
    )
    return final, residual, halos[0]


def program(
    adjoint_start,
    adjoint_source,
    jacobians,
    dissipation,
    wall_mask,
    wake_partner,
    surface_slopes,
    control_points,
    control_weights,
):
    fixed = (adjoint_source, dissipation, wall_mask, wake_partner)
    v, slab, *faces = run_kernel(
        first_faces,
        [shape_of(*d) for d in (TALL, SLAB, FACE, FACE, EDGE)],
        (pltpu.with_memory_space_constraint(adjoint_start, pltpu.HBM),),
        scratch=(pltpu.VMEM(FACE, F32), pltpu.VMEM(FACE, F32), DMA((4,))),
        flops=1000000,
        far=(0,),
    )
    blocks, base = pltpu.with_memory_space_constraint(jacobians, pltpu.HBM), None
    for stage in range(2):
        v, slab, faces, blocks, base = operator_step(
            stage, v, slab, faces, blocks, base, fixed
        )
    kept, bundle = run_kernel(
        surface_sums,
        [shape_of(WRAP // 2, HALF, LANES), shape_of(COMPS + 2, NJ, LANES)],
        (slab, surface_slopes, wall_mask, control_points, control_weights, faces[0]),
        scratch=(
            pltpu.VMEM((6, WRAP, LISTS * ROWS * LANES), BF16),
            pltpu.VMEM((POINT_LANES, LISTS * ROWS * LANES), BF16),
            pltpu.VMEM((WRAP, HALF, LANES), F32),
        ),
        flops=10000000,
        vmem=8,
    )
    faces[0] = bundle
    final, residual, bundle = operator_step(2, v, slab, faces, blocks, base, fixed)
    shape_gradient = reduce_points(kept, bundle)
    return final, residual, shape_gradient


def solution(mesh):
    in_specs = (
        P(None, None, "wrap", "span"),
        P(None, None, "wrap", "span"),
        P(None, None, None, None, "wrap", "span"),
        P(None, "wrap", "span"),
        P("wrap", "span"),
        P("wrap", "span"),
        P(None, None, "wrap", "span"),
        P(None, "wrap", "span"),
        P(None, "wrap", "span"),
    )
    out_specs = (
        P(None, None, "wrap", "span"),
        P(None, None, "wrap", "span"),
        P(None, ("wrap", "span")),
    )
    return jax.shard_map(program, mesh=mesh, in_specs=in_specs, out_specs=out_specs, check_vma=False)
```

```python
import functools

import jax
import jax.numpy as jnp
from jax import lax
from jax.experimental import pallas as pl
from jax.experimental.pallas import tpu as pltpu
from jax.sharding import PartitionSpec as P

COMPS = 5
NJ = 32
ROWS = 16
LANES = 128
HALF = 8
WRAP = 16
SPAN = 8
LISTS = 4
OMEGA = 0.8
F32 = jnp.float32
BF16 = jnp.bfloat16
VSPEC = pl.BlockSpec(memory_space=pltpu.VMEM)


def shape_of(*dims, dtype=F32):
    return jax.ShapeDtypeStruct(dims, dtype)


FARSPEC = pl.BlockSpec(memory_space=pltpu.HBM)


def run_kernel(kernel, outs, args, scratch=(), aliases=None, flops=0, far=(), far_out=(), vmem=4):
    moved = sum(a.size * a.dtype.itemsize for a in args)
    return pl.pallas_call(
        kernel,
        out_shape=outs,
        in_specs=[FARSPEC if n in far else VSPEC for n in range(len(args))],
        out_specs=[FARSPEC if n in far_out else VSPEC for n in range(len(outs))],
        scratch_shapes=list(scratch),
        input_output_aliases=aliases or {},
        compiler_params=pltpu.CompilerParams(vmem_limit_bytes=int(vmem * 2**20)),
        cost_estimate=pl.CostEstimate(flops=flops, transcendentals=0, bytes_accessed=moved),
    )(*args)


def lane_index():
    return lax.broadcasted_iota(jnp.int32, (HALF, LANES), 1)


def row_index():
    return lax.broadcasted_iota(jnp.int32, (HALF, LANES), 0)


def spread(row):
    return jnp.broadcast_to(row, (HALF, LANES))


def pack_edges(packed, halves, j, lane):
    for half in range(2):
        m = 2 * j + half
        here = (lane >> 1) == m
        for c in range(COMPS):
            packed[c] = jnp.where(here, pltpu.roll(halves[c][half], 2 * m + 1, 1), packed[c])
    return packed


def part_faces(low_ref, high_ref, pair_ref, odd_ref):
    even = (lax.axis_index("wrap") & 1) == 0
    low, high = low_ref[:COMPS], high_ref[:COMPS]
    pair_ref[...] = jnp.where(even, high, low)
    odd_ref[...] = jnp.where(even, low, high)


def first_faces(start_ref, v_ref, slab_ref, pair_ref, odd_ref, edge_ref, low_ref, high_ref, sem):
    lane = lane_index()
    copies = []
    for n in range(4):
        at = pl.ds(n * 8, 8)
        copies.append(pltpu.make_async_copy(start_ref.at[:, at], v_ref.at[:, at], sem.at[n]))
        copies[-1].start()
    for c in range(COMPS):
        v_ref[c, NJ] = jnp.zeros((ROWS, LANES), F32)

    def step(j, packed):
        halves = [(v_ref[c, j, :HALF], v_ref[c, j, HALF:]) for c in range(COMPS)]
        for c in range(COMPS):
            low_ref[c, pl.ds(j, 1)] = halves[c][0][:1]
            high_ref[c, pl.ds(j, 1)] = halves[c][1][HALF - 1 :]
        return tuple(pack_edges(list(packed), halves, j, lane))

    packed = tuple(jnp.zeros((HALF, LANES), F32) for _ in range(COMPS))
    for n in range(4):
        copies[n].wait()
        packed = lax.fori_loop(n * 8, n * 8 + 8, step, packed, unroll=8)
    for c in range(COMPS):
        edge_ref[c] = packed[c]
        slab_ref[c] = v_ref[c, 0]
    part_faces(low_ref, high_ref, pair_ref, odd_ref)


def mirror_rows(slab_ref, pair_ref, odd_ref, out_ref):
    even = (lax.axis_index("wrap") & 1) == 0
    for c in range(COMPS):
        pair, odd = pair_ref[c, 0:1], odd_ref[c, 0:1]
        out_ref[c, 0:1] = jnp.where(even, pair, odd)
        for i in range(ROWS):
            out_ref[c, i + 1 : i + 2] = slab_ref[c, ROWS - 1 - i : ROWS - i]
        out_ref[c, ROWS + 1 : ROWS + 2] = jnp.where(even, odd, pair)
        out_ref[c, ROWS + 2 :] = jnp.zeros((24 - ROWS - 2, LANES), F32)


CHUNK = 4
CHUNKS = NJ // CHUNK
PIECE = 2
PIECES = NJ // PIECE
AHEAD = 5


def apply_blocks(stage, *refs):
    last = stage == 2
    *refs, even_stage_ref, odd_stage_ref = refs
    (v_ref, slab_ref, jac_ref, src_ref, dis_ref, near_ref, far_face_ref, pair_ref, odd_ref) = refs[:9]
    if stage == 0:
        out_ref, part_ref, low_ref, high_ref, edge_ref, wide_ref, base_ref = refs[9:16]
        q_ref, before_ref, after_ref, narrow_ref, sems = refs[16:]
    elif stage == 1:
        out_ref, part_ref, low_ref, high_ref, edge_ref, q_ref, before_ref, after_ref = refs[9:]
    else:
        far_ref, part_ref, final_ref, q_ref, before_ref, after_ref, out_ref, sems = refs[9:]

    def block_copy(n):
        at = pl.ds(n * PIECE, PIECE)
        return pltpu.make_async_copy(
            jac_ref.at[:, :, :, at], narrow_ref.at[:, :, :, at], sems.at[n]
        )

    def result_copy(n):
        at = pl.ds(n * CHUNK, CHUNK)
        return pltpu.make_async_copy(out_ref.at[:, at], far_ref.at[:, at], sems.at[n])

    if stage == 0:
        for n in range(AHEAD):
            block_copy(n).start()
    if last:
        final_copies = (
            pltpu.make_async_copy(v_ref.at[:, 1:NJ], final_ref.at[:, 1:], sems.at[CHUNKS]),
            pltpu.make_async_copy(slab_ref, final_ref.at[:, 0], sems.at[CHUNKS + 1]),
        )
        for copy in final_copies:
            copy.start()
    lane, row = lane_index(), row_index()
    place = lax.axis_index("span")
    has_down, has_up = place > 0, place < SPAN - 1
    swapped = (place & 1) == 1
    part_faces(far_face_ref, near_ref, after_ref, before_ref)
    even = (lane & 1) == 0
    for c in range(COMPS):
        up = jnp.where(swapped, odd_ref[c], pair_ref[c])
        down = jnp.where(swapped, pair_ref[c], odd_ref[c])
        from_up = jnp.where(has_up, pltpu.roll(up, LANES - 1, 1), 0.0)
        from_down = jnp.where(has_down, pltpu.roll(down, 1, 1), 0.0)
        q_ref[c] = jnp.where(even, from_up, from_down)
        if not last:
            out_ref[c, NJ] = jnp.zeros((ROWS, LANES), F32)
    first_lane, last_lane = lane == 0, lane == LANES - 1
    first_row, last_row = row == 0, row == HALF - 1

    def plane(c, j):
        if isinstance(j, int) and j < 0:
            return jnp.zeros((ROWS, LANES), F32)
        return slab_ref[c] if isinstance(j, int) and j == 0 else v_ref[c, j]

    def prepare(j, stage_ref):
        for c in range(COMPS):
            here = plane(c, j)
            a, b = here[:HALF], here[HALF:]
            before = spread(before_ref[c, pl.ds(j, 1)])
            after = spread(after_ref[c, pl.ds(j, 1)])
            a_up, b_up = pltpu.roll(a, HALF - 1, 0), pltpu.roll(b, HALF - 1, 0)
            a_dn, b_dn = pltpu.roll(a, 1, 0), pltpu.roll(b, 1, 0)
            next_i = (jnp.where(last_row, b_up, a_up), jnp.where(last_row, after, b_up))
            prev_i = (jnp.where(first_row, before, a_dn), jnp.where(first_row, a_dn, b_dn))
            for half, x in enumerate((a, b)):
                at = slice(half * HALF, (half + 1) * HALF)
                edge = pltpu.roll(q_ref[c], LANES - 1 - 4 * j - 2 * half, 1)
                next_k = jnp.where(last_lane, edge, pltpu.roll(x, LANES - 1, 1))
                prev_k = jnp.where(first_lane, edge, pltpu.roll(x, 1, 1))
                stage_ref[c, at] = next_i[half] - prev_i[half]
                stage_ref[COMPS + c, at] = next_k - prev_k
                stage_ref[2 * COMPS + c, at] = (next_i[half] + prev_i[half]) + (next_k + prev_k)

    def combine(j, stage_ref):
        total = [None] * COMPS
        sums = [None] * COMPS
        for b in range(COMPS):
            below = plane(b, j - 1)
            if last and isinstance(j, int) and j == NJ - 1:
                above = jnp.zeros((ROWS, LANES), F32)
            else:
                above = plane(b, j + 1)
            sums[b] = stage_ref[2 * COMPS + b] + (above + below)
            for d, diff in ((0, stage_ref[b]), (1, above - below), (2, stage_ref[COMPS + b])):
                for c in range(COMPS):
                    if stage == 0:
                        block = narrow_ref[d, c, b, j].astype(F32)
                        wide_ref[d, c, b, j] = block
                        if d == 1 and isinstance(j, int) and j == 0:
                            base_ref[c, b] = block
                    else:
                        block = jac_ref[d, c, b, j]
                    term = block * diff
                    total[c] = term if total[c] is None else total[c] + term
        dis = dis_ref[j]
        weight = None if last else (OMEGA / 6.0) / dis
        for c in range(COMPS):
            x = plane(c, j)
            rhs = src_ref[c, j] - total[c]
            if last:
                rest = rhs - dis * (6.0 * x - sums[c])
            else:
                rest = ((1.0 - OMEGA) * x + (OMEGA / 6.0) * sums[c]) + weight * rhs
            if isinstance(j, int) and j == 0:
                part_ref[c] = rest
            out_ref[c, j] = rest
            if not last:
                low_ref[c, pl.ds(j, 1)] = rest[:1]
                high_ref[c, pl.ds(j, 1)] = rest[ROWS - 1 :]

    def pack(j, packed):
        if last:
            return packed
        halves = [(out_ref[c, j, :HALF], out_ref[c, j, HALF:]) for c in range(COMPS)]
        return tuple(pack_edges(list(packed), halves, j, lane))

    def loop_step(t, packed):
        j = 2 * t + 2
        if stage == 0:

            n = t + 1
            block_copy(n).wait()

            @pl.when(n + AHEAD < PIECES)
            def _():
                block_copy(n + AHEAD).start()

        packed = pack(j - 1, packed)
        prepare(j + 1, odd_stage_ref)
        combine(j, even_stage_ref)
        packed = pack(j, packed)
        prepare(jnp.minimum(j + 2, NJ - 1), even_stage_ref)
        combine(j + 1, odd_stage_ref)
        if last:

            @pl.when(j % CHUNK == CHUNK - 2)
            def _():
                result_copy(j // CHUNK).start()

        return packed

    packed = () if last else tuple(jnp.zeros((HALF, LANES), F32) for _ in range(COMPS))
    if stage == 0:
        block_copy(0).wait()
        block_copy(AHEAD).start()
    prepare(0, even_stage_ref)
    prepare(1, odd_stage_ref)
    combine(0, even_stage_ref)
    packed = pack(0, packed)
    prepare(2, even_stage_ref)
    combine(1, odd_stage_ref)
    packed = lax.fori_loop(0, NJ // 2 - 1, loop_step, packed)
    packed = pack(NJ - 1, packed)
    if last:
        for n in range(CHUNKS):
            result_copy(n).wait()
        for copy in final_copies:
            copy.wait()
    else:
        for c in range(COMPS):
            edge_ref[c] = packed[c]


def add_ghosts(last, *refs):
    (slab_ref, base_ref, dis_ref, wall_ref, partner_ref, window_ref, part_ref) = refs[:7]
    if last:
        _, far_ref, out_ref, sem = refs[7:]
    else:
        low_in, high_in, edge_in, out_ref, pair_ref, odd_ref, edge_ref = refs[7:]
        part_faces(low_in, high_in, pair_ref, odd_ref)
        even = (lax.axis_index("wrap") & 1) == 0
    lane = lane_index()
    base = lax.axis_index("wrap") * ROWS
    row = lax.broadcasted_iota(jnp.int32, (ROWS, LANES), 0)
    shift = partner_ref[...] - (WRAP * ROWS - 1 - base - row)
    wall = wall_ref[...] == 1
    dis = dis_ref[0]
    ghosts = []
    for c in range(COMPS):
        rows = window_ref[c]
        lower, middle, upper = rows[:ROWS], rows[1 : ROWS + 1], rows[2 : ROWS + 2]
        chosen = jnp.where(shift == -1, upper, jnp.where(shift == 1, lower, middle))
        ghosts.append(jnp.where(wall, slab_ref[c], chosen))
    if not last:
        weight = (OMEGA / 6.0) / dis
    for c in range(COMPS):
        total = base_ref[c, 0] * ghosts[0]
        for b in range(1, COMPS):
            total = total + base_ref[c, b] * ghosts[b]
        if last:
            fresh = part_ref[c] + (dis * ghosts[c] + total)
        else:
            fresh = part_ref[c] + ((OMEGA / 6.0) * ghosts[c] + weight * total)
        out_ref[c] = fresh
        if not last:
            low, high = fresh[:1], fresh[ROWS - 1 :]
            pair_ref[c, 0:1] = jnp.where(even, high, low)
            odd_ref[c, 0:1] = jnp.where(even, low, high)
            edge = jnp.where(lane < 2, pltpu.roll(fresh[:HALF], 1, 1), edge_in[c])
            here = (lane == 2) | (lane == 3)
            edge_ref[c] = jnp.where(here, pltpu.roll(fresh[HALF:], 3, 1), edge)
    if last:
        copy = pltpu.make_async_copy(out_ref, far_ref.at[:, 0], sem)
        copy.start()
        copy.wait()


POINT_LANES = 64


def surface_sums(*refs):
    slab_ref, slope_ref, wall_ref, points_ref, weights_ref, face_ref = refs[:6]
    kept_ref, bundle_ref, left_ref, right_ref, sum_ref = refs[6:]
    bundle_ref[:COMPS] = face_ref[...]
    wall = wall_ref[...].astype(F32)
    grads = []
    for x in range(3):
        total = slope_ref[x, 0] * slab_ref[0]
        for a in range(1, COMPS):
            total = total + slope_ref[x, a] * slab_ref[a]
        grads.append(total * wall)
    owner = lax.broadcasted_iota(jnp.int32, (WRAP, LANES), 0)
    inner = lax.broadcasted_iota(jnp.int32, (POINT_LANES, LANES), 0)
    for slot in range(LISTS):
        points = points_ref[slot]
        scale = weights_ref[slot]
        major, minor = points >> 6, points & (POINT_LANES - 1)
        parts = []
        for x in range(3):
            value = grads[x] * scale
            high = value.astype(BF16).astype(F32)
            parts.append((high, value - high))
        for i in range(ROWS):
            at = pl.ds((slot * ROWS + i) * LANES, LANES)
            mine = owner == jnp.broadcast_to(major[i : i + 1], (WRAP, LANES))
            for x in range(3):
                for part in range(2):
                    value = jnp.broadcast_to(parts[x][part][i : i + 1], (WRAP, LANES))
                    left_ref[x * 2 + part, :, at] = jnp.where(mine, value, 0.0).astype(BF16)
            same = inner == jnp.broadcast_to(minor[i : i + 1], (POINT_LANES, LANES))
            right_ref[:, at] = jnp.where(same, 1.0, 0.0).astype(BF16)
    left = left_ref[...].reshape(6 * WRAP, LISTS * ROWS * LANES)
    product = lax.dot_general(
        left, right_ref[...], (((1,), (1,)), ((), ())), preferred_element_type=F32
    )
    sum_ref[...] = jnp.zeros_like(sum_ref)
    for x in range(3):
        first = product[2 * x * WRAP : (2 * x + 1) * WRAP]
        second = product[(2 * x + 1) * WRAP : (2 * x + 2) * WRAP]
        both = first + second
        for w in range(WRAP):
            place = (w & 9) | ((w ^ (w >> 1)) & 2) | (w & 4)
            sum_ref[place, x : x + 1, :POINT_LANES] = both[w : w + 1]
    mine = lax.axis_index("wrap") & 1
    for n in range(WRAP // 2):
        kept_ref[n] = sum_ref[2 * n + mine]
        bundle_ref[COMPS + n // 4, pl.ds(n % 4 * HALF, HALF)] = sum_ref[2 * n + 1 - mine]


def halve_bundle(kept_in, bundle_ref, kept_ref, sent_ref, sum_ref):
    for n in range(WRAP // 2):
        sum_ref[n] = kept_in[n] + bundle_ref[COMPS + n // 4, n % 4 * HALF : (n % 4 + 1) * HALF]
    w = lax.axis_index("wrap")
    deal(((w >> 1) ^ (w >> 2)) & 1, sum_ref, kept_ref, sent_ref)


def halve(kept_in, got_ref, kept_ref, sent_ref, sum_ref):
    sum_ref[...] = kept_in[...] + got_ref[...]
    deal((lax.axis_index("wrap") >> 2) & 1, sum_ref, kept_ref, sent_ref)


def deal(mine, sum_ref, kept_ref, sent_ref):
    for n in range(kept_ref.shape[0]):
        kept_ref[n] = sum_ref[2 * n + mine]
        sent_ref[n] = sum_ref[2 * n + 1 - mine]


def halve_lanes(kept_in, got_ref, kept_ref, sent_ref):
    first, second = kept_in[0] + got_ref[0], kept_in[1] + got_ref[1]
    mine = (lax.axis_index("wrap") >> 3) ^ (lax.axis_index("span") & 1)
    odd = (lane_index() >> 3) & 1
    take = odd == mine
    kept_ref[0] = jnp.where(take, first, second)
    sent_ref[0] = jnp.where(take, second, first)


def add_tiles(a_ref, b_ref, out_ref):
    out_ref[...] = a_ref[...] + b_ref[...]


def finish_points(a_ref, b_ref, c_ref, d_ref, out_ref):
    total = (a_ref[0] + b_ref[0]) + (c_ref[0] + d_ref[0])
    out_ref[...] = pltpu.roll(total, LANES - 8 * lax.axis_index("span"), 1)[:3, :8]


def masked(wrap_mask, span_mask):
    return [
        (w * SPAN + s, (w ^ wrap_mask) * SPAN + (s ^ span_mask))
        for w in range(WRAP)
        for s in range(SPAN)
    ]


FOLDS = (masked(2, 0), masked(6, 0), masked(8, 0), masked(8, 1), masked(0, 2), masked(0, 6), masked(0, 4))


def fold(x, n):
    return lax.ppermute(x, ("wrap", "span"), FOLDS[n - 1])


def reduce_points(kept, bundle):
    tiles = lambda n: [shape_of(n, HALF, LANES)]
    room = lambda n: (pltpu.VMEM((n, HALF, LANES), F32),)
    kept, sent = run_kernel(halve_bundle, tiles(4) * 2, (kept, bundle), scratch=room(8))
    args = (kept, fold(sent, 1))
    kept, sent = run_kernel(halve, tiles(2) * 2, args, scratch=room(4))
    args = (kept, fold(sent, 2))
    kept, sent = run_kernel(halve_lanes, tiles(1) * 2, args)
    got = fold(sent, 3)
    (kept,) = run_kernel(add_tiles, tiles(1), (kept, got))
    got = fold(kept, 4)
    (kept,) = run_kernel(add_tiles, tiles(1), (kept, got))
    others = [fold(kept, n) for n in (5, 6, 7)]
    (out,) = run_kernel(finish_points, [shape_of(3, 8)], (kept, *others))
    return out


WRAP_PAIR = [(i, i ^ 1) for i in range(WRAP)]
WRAP_ODD = [(i, (i + 1) % WRAP if i % 2 else (i - 1) % WRAP) for i in range(WRAP)]
SPAN_PAIR = [(i, i ^ 1) for i in range(SPAN)]


def odd_partner(w, s):
    if s in (0, SPAN - 1):
        return (w ^ 1) * SPAN + s
    return w * SPAN + (s + 1 if s % 2 else s - 1)


SPAN_ODD = [(w * SPAN + s, odd_partner(w, s)) for w in range(WRAP) for s in range(SPAN)]
MIRROR = [(i, WRAP - 1 - i) for i in range(WRAP)]

FIELD = (COMPS, NJ, ROWS, LANES)
TALL = (COMPS, NJ + 1, ROWS, LANES)
SLAB = (COMPS, ROWS, LANES)
STAGE = (3 * COMPS, ROWS, LANES)
FACE = (COMPS, NJ, LANES)
EDGE = (COMPS, HALF, LANES)
BLOCKS = (3, COMPS, COMPS, NJ, ROWS, LANES)
SWEEP_FLOPS = 160 * COMPS * NJ * ROWS * LANES
DMA = pltpu.SemaphoreType.DMA


def exchange(slab, pair_face, odd_face, edge):
    near = lax.ppermute(pair_face, "wrap", WRAP_PAIR)
    far = lax.ppermute(odd_face, "wrap", WRAP_ODD)
    odd = lax.ppermute(edge, ("wrap", "span"), SPAN_ODD)
    pair = lax.ppermute(edge, "span", SPAN_PAIR)
    (rows,) = run_kernel(mirror_rows, [shape_of(COMPS, 24, LANES)], (slab, near, far))
    window = lax.ppermute(rows, "wrap", MIRROR)
    return (near, far, pair, odd), window


def operator_step(stage, v, slab, faces, blocks, base, fixed):
    source, dissipation, wall, partner = fixed
    halos, window = exchange(slab, *faces)
    args = (v, slab, blocks, source, dissipation, *halos)
    kernel = functools.partial(apply_blocks, stage)
    if stage < 2:
        outs = [shape_of(*d) for d in (TALL, SLAB, FACE, FACE, EDGE)]
        scratch = [pltpu.VMEM(EDGE, F32), pltpu.VMEM(FACE, F32), pltpu.VMEM(FACE, F32)]
        if stage == 0:
            outs += [shape_of(*BLOCKS), shape_of(*BLOCKS[1:3], ROWS, LANES)]
            scratch += [pltpu.VMEM(BLOCKS, BF16), DMA((PIECES,))]
        scratch += [pltpu.VMEM(STAGE, F32)] * 2
        v, part, *rest = run_kernel(
            kernel,
            outs,
            args,
            scratch=scratch,
            flops=SWEEP_FLOPS,
            far=(2,) if stage == 0 else (),
            vmem=12 if stage == 0 else 4,
        )
        if stage == 0:
            *rest, blocks, base = rest
        slab, *faces = run_kernel(
            functools.partial(add_ghosts, False),
            [shape_of(*d) for d in (SLAB, FACE, FACE, EDGE)],
            (slab, base, dissipation, wall, partner, window, part, *rest),
            flops=1000000,
        )
        return v, slab, faces, blocks, base
    residual, part, final = run_kernel(
        kernel,
        [shape_of(*FIELD), shape_of(*SLAB), shape_of(*FIELD)],
        args,
        scratch=(
            pltpu.VMEM(EDGE, F32),
            pltpu.VMEM(FACE, F32),
            pltpu.VMEM(FACE, F32),
            pltpu.VMEM(FIELD, F32),
            DMA((CHUNKS + 2,)),
            pltpu.VMEM(STAGE, F32),
            pltpu.VMEM(STAGE, F32),
        ),
        flops=SWEEP_FLOPS,
        far_out=(0, 2),
    )
    (residual,) = run_kernel(
        functools.partial(add_ghosts, True),
        [shape_of(*FIELD)],
        (slab, base, dissipation, wall, partner, window, part, residual),
        scratch=(pltpu.VMEM(SLAB, F32), DMA),
        aliases={7: 0},
        flops=1000000,
        far=(7,),
        far_out=(0,),
    )
    return final, residual, halos[0]


def program(
    adjoint_start,
    adjoint_source,
    jacobians,
    dissipation,
    wall_mask,
    wake_partner,
    surface_slopes,
    control_points,
    control_weights,
):
    fixed = (adjoint_source, dissipation, wall_mask, wake_partner)
    v, slab, *faces = run_kernel(
        first_faces,
        [shape_of(*d) for d in (TALL, SLAB, FACE, FACE, EDGE)],
        (pltpu.with_memory_space_constraint(adjoint_start, pltpu.HBM),),
        scratch=(pltpu.VMEM(FACE, F32), pltpu.VMEM(FACE, F32), DMA((4,))),
        flops=1000000,
        far=(0,),
    )
    blocks, base = pltpu.with_memory_space_constraint(jacobians, pltpu.HBM), None
    for stage in range(2):
        v, slab, faces, blocks, base = operator_step(
            stage, v, slab, faces, blocks, base, fixed
        )
    kept, bundle = run_kernel(
        surface_sums,
        [shape_of(WRAP // 2, HALF, LANES), shape_of(COMPS + 2, NJ, LANES)],
        (slab, surface_slopes, wall_mask, control_points, control_weights, faces[0]),
        scratch=(
            pltpu.VMEM((6, WRAP, LISTS * ROWS * LANES), BF16),
            pltpu.VMEM((POINT_LANES, LISTS * ROWS * LANES), BF16),
            pltpu.VMEM((WRAP, HALF, LANES), F32),
        ),
        flops=10000000,
        vmem=8,
    )
    faces[0] = bundle
    final, residual, bundle = operator_step(2, v, slab, faces, blocks, base, fixed)
    shape_gradient = reduce_points(kept, bundle)
    return final, residual, shape_gradient


def solution(mesh):
    in_specs = (
        P(None, None, "wrap", "span"),
        P(None, None, "wrap", "span"),
        P(None, None, None, None, "wrap", "span"),
        P(None, "wrap", "span"),
        P("wrap", "span"),
        P("wrap", "span"),
        P(None, None, "wrap", "span"),
        P(None, "wrap", "span"),
        P(None, "wrap", "span"),
    )
    out_specs = (
        P(None, None, "wrap", "span"),
        P(None, None, "wrap", "span"),
        P(None, ("wrap", "span")),
    )
    return jax.shard_map(program, mesh=mesh, in_specs=in_specs, out_specs=out_specs, check_vma=False)
```
